32 devices in a mesh: rep: 4 (over y, x), mp: 8 (over z, core).
Axes of the slice: x: 2, y: 2, z: 4, core: 2. Of those that a mesh axis runs over, the one named last changes fastest.
Arguments:
- acts: bfloat16 [1024, 64, 256], P('rep', 'mp'), may hold values from -40 to 40, as said below
- refresh: int32 [64], P(('mp', 'rep')), may hold values from 0 to 8, as said below
- damping: float32 [64], P(('mp', 'rep')), may hold values from 0.2 to 1
- old_inverse: bfloat16 [64, 256, 256], P(('mp', 'rep')), may hold values from -0.375 to 0.375
- grads: bfloat16 [1024, 64, 256], P('rep', 'mp'), may hold values from -6 to 6
Outputs:
- covariance: float32 [64, 256, 256], P(('mp', 'rep'))
- new_inverse: bfloat16 [64, 256, 256], P(('mp', 'rep'))
- precond: bfloat16 [1024, 64, 256], P('rep', 'mp')
The draws below stay inside these ranges and needn't reach their ends.
Inputs may be any that keep to these rules, and one draw needn't show every extreme that they name: `acts`: entries are bfloat16 values of order one with unequal feature scales. Block g * 8 + 2 * r + q (q = 0 or 1) is the q-th block of group g at replica index r. A block is refreshed only by a group through the same r. For every r, each group refreshes exactly one block through r. Of the two blocks of a group at r, at most one is refreshed by another group, and then the other one by the group itself. In every draw some groups refresh a block of another group.
All inputs are finite; a program needn't handle non-finite values. Where the reference program divides by a largest or mean magnitude, that divisor is 1e-20 or more.
Results may differ from the reference program's by a relative error of at most 0.009.
Values may be sent and summed in bfloat16 or wider, within the bound.
A program may use at most 64 MiB of HBM per device.

```python
import math
import jax
import jax.numpy as jnp
from jax import lax

B = 256
OUT = 1024
ITERS = 5
BLK_DEV = 8
GROUPS = 8
TOKENS = 1024
NBLK = 64


def draw_acts(key, part):

    def one_block(block_index):
        block_key = jax.random.fold_in(jax.random.fold_in(key, 7), block_index)
        key_list = jax.random.split(block_key, 3)
        base_noise = jax.random.normal(key_list[0], (TOKENS, B), jnp.float32)
        scales = jnp.exp(jax.random.uniform(key_list[2], (B,), jnp.float32, jnp.log(0.5), jnp.log(2.0)))
        feature_order = jax.random.permutation(key_list[1], B)
        mixed = base_noise + 0.7 * jnp.take(base_noise, feature_order, axis=1)
        return (mixed * scales[None, :]).astype(jnp.bfloat16)
    blocks = lax.map(one_block, jnp.arange(NBLK, dtype=jnp.int32))
    return jnp.transpose(blocks, (1, 0, 2))


def draw_refresh(key, part):
    replicas = BLK_DEV // 2
    heavy_count = GROUPS * 3 // 8
    key_list = jax.random.split(jax.random.fold_in(key, 23), 2)
    row_keys = jax.random.split(key_list[0], replicas)
    arranged = jax.vmap(lambda row_key: jax.random.permutation(row_key, GROUPS))(row_keys).astype(jnp.int32)
    position = jnp.argsort(arranged, axis=1, stable=True).astype(jnp.int32)
    local_pick = jax.random.randint(key_list[1], (replicas, GROUPS), 0, 2)
    partner = jnp.take_along_axis(arranged, jnp.minimum(position + heavy_count, GROUPS - 1), axis=1)
    own_group = jnp.broadcast_to(jnp.arange(GROUPS, dtype=jnp.int32)[None, :], (replicas, GROUPS))
    is_giver = position < heavy_count
    is_taker = (position >= heavy_count) & (position < 2 * heavy_count)
    other_value = jnp.where(is_giver, partner, GROUPS)
    first_value = jnp.where(local_pick == 0, own_group, other_value)
    second_value = jnp.where(local_pick == 1, own_group, other_value)
    first_value = jnp.where(is_taker, GROUPS, first_value)
    second_value = jnp.where(is_taker, GROUPS, second_value)
    stacked = jnp.stack([first_value, second_value], axis=-1)
    return jnp.transpose(stacked, (1, 0, 2)).reshape(NBLK).astype(jnp.int32)


def levels(rng, shape, cuts, least, top_value):
    gain = 1.0
    for dim, shards_of in cuts:
        heights = jax.random.uniform(jax.random.fold_in(jax.random.fold_in(rng, 6), dim), (shards_of,), jnp.float32, least / len(cuts), top_value / len(cuts))
        gain = gain * jnp.repeat(jnp.exp(heights), shape[dim] // shards_of).reshape((-1,) + (1,) * (len(shape) - 1 - dim))
    return gain


def scatter_about(stream_key, shape, width, most, cuts=(), kind=jnp.bfloat16):
    factor_of = levels(stream_key, shape, cuts, -0.22, 0.18) if cuts else 1.0
    values = jax.random.normal(stream_key, shape, jnp.float32) * width * factor_of
    return jnp.minimum(jnp.maximum(values, -most), most).astype(kind)


def setup_inputs(seed: int = 0) -> dict:
    arg_keys = jax.random.split(jax.random.key(seed), 6)
    return {
        "acts": draw_acts(jax.random.fold_in(arg_keys[5], 71), 0),
        "refresh": draw_refresh(jax.random.fold_in(arg_keys[5], 71), 0),
        "damping": jnp.clip(jnp.exp(math.log(1.0) - 1.609438 * jax.random.uniform(arg_keys[2], (NBLK,), jnp.float32) ** levels(arg_keys[2], (NBLK,), ((0, 32),), -0.2, 0.2)), 0.2, 1.0),
        "old_inverse": scatter_about(arg_keys[3], (NBLK, B, B), B ** -0.5, 0.375, ((0, 32),)),
        "grads": scatter_about(arg_keys[4], (OUT, NBLK, B), 1.0, 6.0, ((0, 4), (1, 8))),
    }


HIGHEST_PRECISION = lax.Precision.HIGHEST


def newton_inverse(gram, damp_value):
    order_size = gram.shape[-1]
    identity = jnp.eye(order_size, dtype=jnp.float32)
    matrix = gram + damp_value * identity
    row_bound = jnp.max(jnp.sum(jnp.abs(matrix), axis=1))
    approx = identity / row_bound
    for iteration in range(ITERS):
        product = jnp.dot(matrix, approx, precision=HIGHEST_PRECISION, preferred_element_type=jnp.float32)
        approx = jnp.dot(approx, 2.0 * identity - product, precision=HIGHEST_PRECISION, preferred_element_type=jnp.float32)
    return approx


def reference(acts, refresh, damping, old_inverse, grads):
    def block_gram(block_index):
        block_acts = lax.dynamic_index_in_dim(acts, block_index, 1, keepdims=False)
        return jnp.dot(block_acts.T, block_acts, preferred_element_type=jnp.float32) / TOKENS

    covariance = lax.map(block_gram, jnp.arange(NBLK, dtype=jnp.int32))

    def invert_one(inputs_pair):
        return newton_inverse(inputs_pair[0], inputs_pair[1]).astype(jnp.bfloat16)

    refreshed = lax.map(invert_one, (covariance, damping))
    due_mask = refresh != GROUPS
    new_inverse = jnp.where(due_mask[:, None, None], refreshed, old_inverse)

    def precondition(block_index):
        grad_block = lax.dynamic_index_in_dim(grads, block_index, 1, keepdims=False)
        inverse = lax.dynamic_index_in_dim(new_inverse, block_index, 0, keepdims=False)
        return jnp.dot(grad_block, inverse, preferred_element_type=jnp.float32).astype(jnp.bfloat16)

    precond = lax.map(precondition, jnp.arange(NBLK, dtype=jnp.int32))
    return covariance, new_inverse, jnp.transpose(precond, (1, 0, 2))
```

```python
import functools
import math

import jax
import jax.numpy as jnp
from jax import lax
from jax.experimental import pallas as pl
from jax.experimental.pallas import tpu as pltpu
from jax.sharding import PartitionSpec as P

ITERS = 5
CHUNKS = 4
LOADS = 4
MESH = pl.DeviceIdType.MESH
F32 = jnp.float32
BF16 = jnp.bfloat16


def split(x):
    high = x.astype(BF16)
    return high, (x - high.astype(F32)).astype(BF16)


def dot3(lhs, rhs):
    lh, ll = lhs
    rh, rl = rhs
    mm = functools.partial(jnp.dot, preferred_element_type=F32)
    return mm(lh, rh) + (mm(lh, rl) + mm(ll, rh))


def partner(me, step, n):
    if n & (n - 1):
        return lax.rem(me + step, n), lax.rem(me + n - step, n)
    other = me
    bit = 1
    while bit < n:
        if step & bit:
            other = other + bit * (1 - 2 * lax.rem(me // bit, 2))
        bit *= 2
    return other, other


def general_kernel(
    n,
    held,
    groups,
    tokens_all,
    acts_hbm,
    refresh_ref,
    damping_ref,
    old_hbm,
    grads_hbm,
    cov_ref,
    inv_ref,
    pre_f,
    acts_v,
    grads_v,
    old_v,
    acts_f,
    grads_f,
    own_f,
    out_buf,
    in_buf,
    gathered,
    load_sem,
    rs_send,
    rs_recv,
    ag_send,
    ag_recv,
):
    me = lax.axis_index("rep")
    blocks = n * held
    order = inv_ref.shape[-1]
    half = order // 2
    rows = acts_v.shape[0] // blocks

    barrier = pltpu.get_barrier_semaphore()
    for step in range(1, n):
        pl.semaphore_signal(
            barrier, inc=1, device_id={"rep": partner(me, step, n)[0]}, device_id_type=MESH
        )

    piece = acts_v.shape[0] // LOADS
    loads = [
        pltpu.make_async_copy(acts_hbm.at[pl.ds(c * piece, piece)], acts_v.at[pl.ds(c * piece, piece)], load_sem.at[3 + c])
        for c in range(LOADS)
    ] + [
        pltpu.make_async_copy(grads_hbm, grads_v, load_sem.at[1]),
        pltpu.make_async_copy(old_hbm, old_v, load_sem.at[2]),
    ]
    for load in loads:
        load.start()

    row_id = lax.broadcasted_iota(jnp.int32, (half, half), 0)
    col_id = lax.broadcasted_iota(jnp.int32, (half, half), 1)
    upper = col_id >= row_id
    on_diag = col_id == row_id

    def widen(source, target):
        for tile in range(order // 128):
            target[tile] = source[:, tile * 128 : (tile + 1) * 128].astype(F32)

    def take(source, block):
        return jnp.concatenate(
            [
                source[tile, pl.ds(block, rows, stride=blocks), :]
                for tile in range(order // 128)
            ],
            axis=1,
        ).astype(BF16)

    def gram(block):
        part = take(acts_f, block)
        full = lax.dot_general(
            part, part, (((0,), (0,)), ((), ())), preferred_element_type=F32
        )
        low = full[half:, half:]
        last = jnp.sum(jnp.where(on_diag, low, 0.0), axis=0, keepdims=True)
        return full[:half, half:], jnp.where(upper, full[:half, :half], low), last

    for c in range(LOADS):
        loads[c].wait()
        part = pl.ds(c * piece, piece)
        for tile in range(order // 128):
            acts_f[tile, part, :] = acts_v[part, tile * 128 : (tile + 1) * 128].astype(F32)

    rs = {}
    greeted = False
    steps = list(range(n - 1, 0, -1))
    for slot in range(held):
        for step in steps:
            target = partner(me, step, n)[0]
            cross, packed, last = gram(target * held + slot)
            place = out_buf.at[step - 1, slot]
            place[:half, :] = cross.astype(BF16)
            place[half : 2 * half, :] = packed.astype(BF16)
            place[2 * half :, :] = jnp.broadcast_to(last, (16, half)).astype(BF16)
            if not greeted:
                pl.semaphore_wait(barrier, n - 1)
                greeted = True
            copy = pltpu.make_async_remote_copy(
                src_ref=place,
                dst_ref=in_buf.at[step - 1, slot],
                send_sem=rs_send.at[step - 1, slot],
                recv_sem=rs_recv.at[step - 1, slot],
                device_id={"rep": target},
                device_id_type=MESH,
            )
            copy.start()
            rs[step, slot] = copy
        cross, packed, last = gram(me * held + slot)
        own_f[slot, :half, :] = cross
        own_f[slot, half : 2 * half, :] = packed
        own_f[slot, 2 * half :, :] = jnp.broadcast_to(last, (8, half))

    loads[LOADS].wait()
    widen(grads_v, grads_f)
    loads[LOADS + 1].wait()

    eye = jnp.where(
        lax.broadcasted_iota(jnp.int32, (order, order), 0)
        == lax.broadcasted_iota(jnp.int32, (order, order), 1),
        1.0,
        0.0,
    ).astype(F32)

    ag = {}

    def ship(key, source, target, step, sem):
        copy = pltpu.make_async_remote_copy(
            src_ref=source,
            dst_ref=target,
            send_sem=ag_send.at[sem],
            recv_sem=ag_recv.at[sem],
            device_id={"rep": partner(me, step, n)[0]},
            device_id_type=MESH,
        )
        copy.start()
        ag[key] = copy

    def refresh_block(slot):
        total = own_f[slot]
        total_cross, total_packed, total_last = (
            total[:half],
            total[half : 2 * half],
            total[2 * half : 2 * half + 1],
        )
        for step in steps:
            rs[step, slot].wait_recv()
            came = in_buf[step - 1, slot].astype(F32)
            total_cross = total_cross + came[:half]
            total_packed = total_packed + came[half : 2 * half]
            total_last = total_last + came[2 * half : 2 * half + 1]
        scale = 1.0 / tokens_all
        flipped = total_packed.T
        first = jnp.where(upper, total_packed, flipped)
        second = jnp.where(
            on_diag,
            jnp.broadcast_to(total_last, (half, half)),
            jnp.where(upper, flipped, total_packed),
        )
        covariance = (
            jnp.concatenate(
                [
                    jnp.concatenate([first, total_cross], axis=1),
                    jnp.concatenate([total_cross.T, second], axis=1),
                ],
                axis=0,
            )
            * scale
        )
        cov_ref[slot] = covariance
        matrix = covariance + damping_ref[slot] * eye
        bound = jnp.max(jnp.sum(jnp.abs(matrix), axis=0, keepdims=True), axis=1, keepdims=True)
        inverse_bound = 1.0 / bound
        residual = eye - matrix * inverse_bound
        series = eye + residual
        power = split(residual)
        power = split(dot3(power, power))
        for iteration in range(2, ITERS):
            left = split(series)
            square = dot3(power, power)
            series = series + dot3(left, power)
            power = split(square)
        series = series + dot3(split(series), power)
        approx = (series * inverse_bound).astype(BF16)
        due = jnp.full((order, order), refresh_ref[slot], jnp.int32) != groups
        chosen = jnp.where(due, approx, old_v[slot])
        inv_ref[slot] = chosen
        gathered[0, slot] = chosen
        for step in steps:
            ship(
                (slot, step),
                gathered.at[0, slot],
                gathered.at[step, slot],
                step,
                slot * n + step,
            )

    def apply(step, slot):
        block = partner(me, step, n)[1] * held + slot
        result = jnp.dot(
            take(grads_f, block), gathered[step, slot], preferred_element_type=F32
        )
        for tile in range(order // 128):
            pre_f[tile, pl.ds(block, rows, stride=blocks), :] = result[
                :, tile * 128 : (tile + 1) * 128
            ]

    for slot in range(held):
        refresh_block(slot)
    for slot in range(held):
        apply(0, slot)
    for slot in range(held):
        for step in steps:
            ag[slot, step].wait_recv()
            apply(step, slot)
    for copy in rs.values():
        copy.wait_send()
    for copy in ag.values():
        copy.wait_send()


def square_kernel(
    held,
    groups,
    tokens_all,
    acts_hbm,
    refresh_hbm,
    damping_hbm,
    old_hbm,
    grads_hbm,
    cov_ref,
    inv_ref,
    pre_f,
    refresh_s,
    damping_s,
    acts_v,
    grads_v,
    old_v,
    acts_f,
    grads_f,
    grads_b,
    own_f,
    mid_f,
    sum_out,
    sum_in,
    early_own,
    early_in,
    late_own,
    late_in,
    load_sem,
    send_sem,
    recv_sem,
):
    n = 4
    me = lax.axis_index("rep")
    blocks = n * held
    order = inv_ref.shape[-1]
    half = order // 2
    rows = acts_v.shape[0] // blocks
    grad_rows = grads_v.shape[0] // blocks
    peer = [partner(me, step, n)[0] for step in range(n)]

    barrier = pltpu.get_barrier_semaphore()
    for step in (1, 2):
        pl.semaphore_signal(
            barrier, inc=1, device_id={"rep": peer[step]}, device_id_type=MESH
        )

    piece = acts_v.shape[0] // LOADS
    acts_loads = [
        pltpu.make_async_copy(
            acts_hbm.at[pl.ds(c * piece, piece)],
            acts_v.at[pl.ds(c * piece, piece)],
            load_sem.at[4 + c],
        )
        for c in range(LOADS)
    ]
    old_load = pltpu.make_async_copy(old_hbm, old_v, load_sem.at[0])
    grads_load = pltpu.make_async_copy(grads_hbm, grads_v, load_sem.at[1])
    refresh_load = pltpu.make_async_copy(refresh_hbm, refresh_s, load_sem.at[2])
    damping_load = pltpu.make_async_copy(damping_hbm, damping_s, load_sem.at[3])
    for load in acts_loads + [old_load, refresh_load, damping_load, grads_load]:
        load.start()

    copies = {}

    def send(key, source, target, step):
        index = len(copies)
        copy = pltpu.make_async_remote_copy(
            src_ref=source,
            dst_ref=target,
            send_sem=send_sem.at[index],
            recv_sem=recv_sem.at[index],
            device_id={"rep": peer[step]},
            device_id_type=MESH,
        )
        copy.start()
        copies[key] = copy

    def arrived(*key):
        copies[key].wait_recv()

    row_id = lax.broadcasted_iota(jnp.int32, (half, half), 0)
    col_id = lax.broadcasted_iota(jnp.int32, (half, half), 1)
    upper = col_id >= row_id
    on_diag = col_id == row_id

    def widen(source, target, part):
        for tile in range(order // 128):
            target[tile, part, :] = source[part, tile * 128 : (tile + 1) * 128].astype(F32)

    def take(source, block, count):
        return jnp.concatenate(
            [
                source[tile, pl.ds(block, count, stride=blocks), :]
                for tile in range(order // 128)
            ],
            axis=1,
        ).astype(BF16)

    def diagonal(square):
        return jnp.sum(jnp.where(on_diag, square, 0.0), axis=0, keepdims=True)

    def gram(block):
        part = take(acts_f, block, rows)
        full = lax.dot_general(
            part, part, (((0,), (0,)), ((), ())), preferred_element_type=F32
        )
        low = full[half:, half:]
        return full[:half, half:], jnp.where(upper, full[:half, :half], low), diagonal(low)

    def keep(place, parts):
        cross, packed, last = parts
        place[:half, :] = cross.astype(place.dtype)
        place[half : 2 * half, :] = packed.astype(place.dtype)
        place[2 * half :, :] = jnp.broadcast_to(
            last, (place.shape[0] - 2 * half, half)
        ).astype(place.dtype)

    def parts_of(value):
        value = value.astype(F32)
        return value[:half], value[half : 2 * half], value[2 * half : 2 * half + 1]

    def add(*terms):
        return tuple(sum(entries[1:], entries[0]) for entries in zip(*terms))

    def axes(slot):
        return (1, 2) if slot % 2 == 0 else (2, 1)

    whole, first_half, last_half = pl.ds(0, half), pl.ds(0, half // 2), pl.ds(half // 2, half // 2)
    packed_whole = pl.ds(half, half)
    packed_first, packed_last = pl.ds(half, half // 2), pl.ds(half + half // 2, half // 2)

    def early_relay(kind, slot, first, last):
        arrived(kind, slot, 1)
        send((kind, slot, "y"), early_in.at[0, slot, first], early_in.at[2, slot, first], 2)
        arrived(kind, slot, 2)
        send((kind, slot, "x"), early_in.at[1, slot, last], early_in.at[2, slot, last], 1)

    pl.semaphore_wait(barrier, 2)
    for slot in range(held):
        for step in (1, 2):
            send(
                ("d", slot, step),
                old_hbm.at[slot, pl.ds(half, half), pl.ds(0, half)],
                early_in.at[step - 1, slot, whole],
                step,
            )

    for c in range(LOADS):
        acts_loads[c].wait()
        widen(acts_v, acts_f, pl.ds(c * piece, piece))

    for stage in (0, 1):
        for slot in range(held):
            near, far = axes(slot)
            block = peer[3 if stage == 0 else near] * held + slot
            keep(sum_out.at[slot, stage], gram(block))
            send(("s", slot, stage), sum_out.at[slot, stage], sum_in.at[slot, stage], near)
    for slot in range(held):
        keep(mid_f.at[slot], gram(peer[axes(slot)[1]] * held + slot))
    for slot in range(held):
        keep(own_f.at[slot], gram(me * held + slot))

    old_load.wait()
    for slot in range(held):
        old = old_v[slot].astype(F32)
        early_own[slot] = jnp.where(upper, old[half:, half:], old[:half, :half]).astype(BF16)

    for slot in range(held):
        arrived("s", slot, 0)
        keep(sum_out.at[slot, 2], add(parts_of(mid_f[slot]), parts_of(sum_in[slot, 0])))
        send(("s", slot, 2), sum_out.at[slot, 2], sum_in.at[slot, 2], axes(slot)[1])

    for slot in range(held):
        early_relay("d", slot, first_half, last_half)
    for slot in range(held):
        for step in (1, 2):
            send(
                ("e", slot, step), early_own.at[slot], early_in.at[step - 1, slot, packed_whole], step
            )

    grads_load.wait()
    widen(grads_v, grads_f, pl.ds(0, grads_v.shape[0]))
    for step in range(n):
        for slot in range(held):
            grads_b[step * held + slot] = take(grads_f, peer[step] * held + slot, grad_rows)

    eye = jnp.where(
        lax.broadcasted_iota(jnp.int32, (order, order), 0)
        == lax.broadcasted_iota(jnp.int32, (order, order), 1),
        1.0,
        0.0,
    ).astype(F32)
    refresh_load.wait()
    damping_load.wait()

    cut = (order + 16) // 32 * 16
    top, bottom = pl.ds(0, cut), pl.ds(cut, order + 16 - cut)

    def refresh_block(slot):
        arrived("s", slot, 1)
        arrived("s", slot, 2)
        cross, packed, last = add(
            parts_of(own_f[slot]), parts_of(sum_in[slot, 1]), parts_of(sum_in[slot, 2])
        )
        scale = 1.0 / tokens_all
        flipped = packed.T
        first = jnp.where(upper, packed, flipped)
        second = jnp.where(
            on_diag,
            jnp.broadcast_to(last, (half, half)),
            jnp.where(upper, flipped, packed),
        )
        covariance = (
            jnp.concatenate(
                [
                    jnp.concatenate([first, cross], axis=1),
                    jnp.concatenate([cross.T, second], axis=1),
                ],
                axis=0,
            )
            * scale
        )
        cov_ref[slot] = covariance
        matrix = covariance + damping_s[slot] * eye
        bound = jnp.max(jnp.sum(jnp.abs(matrix), axis=0, keepdims=True), axis=1, keepdims=True)
        inverse_bound = 1.0 / bound
        residual = eye - matrix * inverse_bound
        series = eye + residual
        power = split(residual)
        power = split(dot3(power, power))
        for iteration in range(2, ITERS):
            left = split(series)
            square = dot3(power, power)
            series = series + dot3(left, power)
            power = split(square)
        series = series + dot3(split(series), power)
        approx = (series * inverse_bound).astype(BF16)
        due = jnp.full((order, order), refresh_s[slot], jnp.int32) != groups
        chosen = jnp.where(due, approx, old_v[slot])
        inv_ref[slot] = chosen
        chosen = chosen.astype(F32)
        low = chosen[half:, half:]
        late_own[slot, :half, :] = chosen[:half, half:].astype(BF16)
        late_own[slot, half:order, :] = jnp.where(upper, chosen[:half, :half], low).astype(BF16)
        due_row = jnp.where(jnp.full((8, half), refresh_s[slot], jnp.int32) != groups, 1.0, 0.0)
        late_own[slot, order:, :] = jnp.concatenate(
            [jnp.broadcast_to(diagonal(low), (8, half)), due_row], axis=0
        ).astype(BF16)

    def late_first(slot):
        send(("l", slot, 1, "top"), late_own.at[slot, top], late_in.at[0, slot, top], 1)
        send(("l", slot, 2, "bottom"), late_own.at[slot, bottom], late_in.at[1, slot, bottom], 2)

    def late_rest(slot):
        send(("l", slot, 1, "bottom"), late_own.at[slot, bottom], late_in.at[0, slot, bottom], 1)
        send(("l", slot, 2, "top"), late_own.at[slot, top], late_in.at[1, slot, top], 2)

    def late_relay(slot):
        arrived("l", slot, 1, "top")
        send(("l", slot, 3, "top"), late_in.at[0, slot, top], late_in.at[2, slot, top], 2)
        arrived("l", slot, 2, "bottom")
        send(("l", slot, 3, "bottom"), late_in.at[1, slot, bottom], late_in.at[2, slot, bottom], 1)

    def multiply(step, slot, inverse):
        block = peer[step] * held + slot
        result = jnp.dot(grads_b[step * held + slot], inverse, preferred_element_type=F32)
        for tile in range(order // 128):
            pre_f[tile, pl.ds(block, grad_rows, stride=blocks), :] = result[
                :, tile * 128 : (tile + 1) * 128
            ]

    def apply(step, slot):
        late = late_in[step - 1, slot].astype(F32)
        early = early_in[step - 1, slot].astype(F32)
        cross, packed = late[:half], late[half:order]
        last, flag = late[order : order + 1], late[order + 8 : order + 9]
        due = jnp.broadcast_to(flag, (half, half)) > 0.5
        other = jnp.where(
            due,
            jnp.where(on_diag, jnp.broadcast_to(last, (half, half)), packed.T),
            early[half:],
        )
        inverse = jnp.concatenate(
            [
                jnp.concatenate([jnp.where(upper, packed, other), cross], axis=1),
                jnp.concatenate(
                    [jnp.where(due, cross.T, early[:half]), jnp.where(upper, other, packed)], axis=1
                ),
            ],
            axis=0,
        ).astype(BF16)
        multiply(step, slot, inverse)

    for slot in range(held):
        refresh_block(slot)
        late_first(slot)
        early_relay("e", slot, packed_first, packed_last)
        if slot > 0:
            late_relay(slot - 1)
        late_rest(slot)
    for slot in range(held):
        multiply(0, slot, inv_ref[slot])
    late_relay(held - 1)
    for kind in ("d", "e"):
        for slot in range(held):
            arrived(kind, slot, "x")
            arrived(kind, slot, "y")
    for slot in range(held):
        arrived("l", slot, 1, "bottom")
        apply(1, slot)
        arrived("l", slot, 2, "top")
        apply(2, slot)
        arrived("l", slot, 3, "top")
        arrived("l", slot, 3, "bottom")
        apply(3, slot)
    for copy in copies.values():
        copy.wait_send()


def deliver(cov_v, inv_v, wide, cov_hbm, inv_hbm, pre_hbm, narrow, sem):
    copies = [
        pltpu.make_async_copy(cov_v, cov_hbm, sem.at[0]),
        pltpu.make_async_copy(inv_v, inv_hbm, sem.at[1]),
    ]
    for copy in copies:
        copy.start()
    size = narrow.shape[0] // CHUNKS
    for chunk in range(CHUNKS):
        part = pl.ds(chunk * size, size)
        for tile in range(wide.shape[0]):
            narrow[part, tile * 128 : (tile + 1) * 128] = wide[tile, part, :].astype(BF16)
        copy = pltpu.make_async_copy(narrow.at[part], pre_hbm.at[part], sem.at[2 + chunk])
        copy.start()
        copies.append(copy)
    for copy in copies:
        copy.wait()


def local(acts, refresh, damping, old_inverse, grads):
    n = lax.axis_size("rep")
    groups = lax.axis_size("mp")
    rows, blocks, order = acts.shape
    grad_rows = grads.shape[0]
    held = refresh.shape[0]
    half = order // 2
    tiles = order // 128
    any_space = pl.BlockSpec(memory_space=pltpu.HBM)
    smem = pl.BlockSpec(memory_space=pltpu.SMEM)
    vmem = pl.BlockSpec(memory_space=pltpu.VMEM)
    wide_scratch = [
        pltpu.VMEM((rows * blocks, order), BF16),
        pltpu.VMEM((grad_rows * blocks, order), BF16),
        pltpu.VMEM((held, order, order), BF16),
        pltpu.VMEM((tiles, rows * blocks, 128), F32),
        pltpu.VMEM((tiles, grad_rows * blocks, 128), F32),
    ]
    if n == 4:
        body = functools.partial(square_kernel, held, groups, rows * n)
        scratch = (
            [pltpu.SMEM((held,), jnp.int32), pltpu.SMEM((held,), F32)]
            + wide_scratch
            + [
                pltpu.VMEM((blocks, grad_rows, order), BF16),
                pltpu.VMEM((held, order + 8, half), F32),
                pltpu.VMEM((held, order + 8, half), F32),
                pltpu.VMEM((held, 3, order + 16, half), BF16),
                pltpu.VMEM((held, 3, order + 16, half), BF16),
                pltpu.VMEM((held, half, half), BF16),
                pltpu.VMEM((3, held, order, half), BF16),
                pltpu.VMEM((held, order + 16, half), BF16),
                pltpu.VMEM((3, held, order + 16, half), BF16),
                pltpu.SemaphoreType.DMA((4 + LOADS,)),
                pltpu.SemaphoreType.DMA((17 * held,)),
                pltpu.SemaphoreType.DMA((17 * held,)),
            ]
        )
        small = any_space
    else:
        body = functools.partial(general_kernel, n, held, groups, rows * n)
        scratch = wide_scratch + [
            pltpu.VMEM((held, order + 8, half), F32),
            pltpu.VMEM((n - 1, held, order + 16, half), BF16),
            pltpu.VMEM((n - 1, held, order + 16, half), BF16),
            pltpu.VMEM((n, held, order, order), BF16),
            pltpu.SemaphoreType.DMA((3 + LOADS,)),
            pltpu.SemaphoreType.DMA((n - 1, held)),
            pltpu.SemaphoreType.DMA((n - 1, held)),
            pltpu.SemaphoreType.DMA((held * n,)),
            pltpu.SemaphoreType.DMA((held * n,)),
        ]
        small = smem
    need = sum(
        math.prod(item.shape) * jnp.dtype(item.dtype).itemsize
        for item in scratch
        if item.memory_space == pltpu.VMEM
    )
    covariance, new_inverse, wide = pl.pallas_call(
        body,
        out_shape=(
            pltpu.VMEM((held, order, order), F32),
            pltpu.VMEM((held, order, order), BF16),
            pltpu.VMEM((tiles, grad_rows * blocks, 128), F32),
        ),
        in_specs=[any_space, small, small, any_space, any_space],
        out_specs=(vmem, vmem, vmem),
        scratch_shapes=scratch,
        compiler_params=pltpu.CompilerParams(
            collective_id=0, has_side_effects=True, vmem_limit_bytes=need + (8 << 20)
        ),
    )(
        pltpu.with_memory_space_constraint(acts.reshape(rows * blocks, order), pltpu.HBM),
        pltpu.with_memory_space_constraint(refresh, pltpu.HBM),
        pltpu.with_memory_space_constraint(damping, pltpu.HBM),
        pltpu.with_memory_space_constraint(old_inverse, pltpu.HBM),
        pltpu.with_memory_space_constraint(grads.reshape(grad_rows * blocks, order), pltpu.HBM),
    )
    covariance, new_inverse, precond = pl.pallas_call(
        deliver,
        out_shape=(
            jax.ShapeDtypeStruct((held, order, order), F32),
            jax.ShapeDtypeStruct((held, order, order), BF16),
            jax.ShapeDtypeStruct((grad_rows * blocks, order), BF16),
        ),
        in_specs=[vmem] * 3,
        out_specs=(any_space,) * 3,
        scratch_shapes=[
            pltpu.VMEM((grad_rows * blocks, order), BF16),
            pltpu.SemaphoreType.DMA((2 + CHUNKS,)),
        ],
        compiler_params=pltpu.CompilerParams(
            vmem_limit_bytes=grad_rows * blocks * order * 2 + (2 << 20)
        ),
    )(covariance, new_inverse, wide)
    return covariance, new_inverse, precond.reshape(grad_rows, blocks, order)


def solution(mesh):
    return jax.shard_map(
        local,
        mesh=mesh,
        in_specs=(
            P("rep", "mp", None),
            P(("mp", "rep")),
            P(("mp", "rep")),
            P(("mp", "rep"), None, None),
            P("rep", "mp", None),
        ),
        out_specs=(
            P(("mp", "rep"), None, None),
            P(("mp", "rep"), None, None),
            P("rep", "mp", None),
        ),
        check_vma=False,
    )
```

```python
import functools
import math

import jax
import jax.numpy as jnp
from jax import lax
from jax.experimental import pallas as pl
from jax.experimental.pallas import tpu as pltpu
from jax.sharding import PartitionSpec as P

ITERS = 5
CHUNKS = 4
LOADS = 4
MESH = pl.DeviceIdType.MESH
F32 = jnp.float32
BF16 = jnp.bfloat16


def split(x):
    high = x.astype(BF16)
    return high, (x - high.astype(F32)).astype(BF16)


def dot3(lhs, rhs):
    lh, ll = lhs
    rh, rl = rhs
    mm = functools.partial(jnp.dot, preferred_element_type=F32)
    return mm(lh, rh) + (mm(lh, rl) + mm(ll, rh))


def partner(me, step, n):
    if n & (n - 1):
        return lax.rem(me + step, n), lax.rem(me + n - step, n)
    other = me
    bit = 1
    while bit < n:
        if step & bit:
            other = other + bit * (1 - 2 * lax.rem(me // bit, 2))
        bit *= 2
    return other, other


def general_kernel(
    n,
    held,
    groups,
    tokens_all,
    acts_hbm,
    refresh_ref,
    damping_ref,
    old_hbm,
    grads_hbm,
    cov_ref,
    inv_ref,
    pre_f,
    acts_v,
    grads_v,
    old_v,
    acts_f,
    grads_f,
    own_f,
    out_buf,
    in_buf,
    gathered,
    load_sem,
    rs_send,
    rs_recv,
    ag_send,
    ag_recv,
):
    me = lax.axis_index("rep")
    blocks = n * held
    order = inv_ref.shape[-1]
    half = order // 2
    rows = acts_v.shape[0] // blocks

    barrier = pltpu.get_barrier_semaphore()
    for step in range(1, n):
        pl.semaphore_signal(
            barrier, inc=1, device_id={"rep": partner(me, step, n)[0]}, device_id_type=MESH
        )

    piece = acts_v.shape[0] // LOADS
    loads = [
        pltpu.make_async_copy(acts_hbm.at[pl.ds(c * piece, piece)], acts_v.at[pl.ds(c * piece, piece)], load_sem.at[3 + c])
        for c in range(LOADS)
    ] + [
        pltpu.make_async_copy(grads_hbm, grads_v, load_sem.at[1]),
        pltpu.make_async_copy(old_hbm, old_v, load_sem.at[2]),
    ]
    for load in loads:
        load.start()

    row_id = lax.broadcasted_iota(jnp.int32, (half, half), 0)
    col_id = lax.broadcasted_iota(jnp.int32, (half, half), 1)
    upper = col_id >= row_id
    on_diag = col_id == row_id

    def widen(source, target):
        for tile in range(order // 128):
            target[tile] = source[:, tile * 128 : (tile + 1) * 128].astype(F32)

    def take(source, block):
        return jnp.concatenate(
            [
                source[tile, pl.ds(block, rows, stride=blocks), :]
                for tile in range(order // 128)
            ],
            axis=1,
        ).astype(BF16)

    def gram(block):
        part = take(acts_f, block)
        full = lax.dot_general(
            part, part, (((0,), (0,)), ((), ())), preferred_element_type=F32
        )
        low = full[half:, half:]
        last = jnp.sum(jnp.where(on_diag, low, 0.0), axis=0, keepdims=True)
        return full[:half, half:], jnp.where(upper, full[:half, :half], low), last

    for c in range(LOADS):
        loads[c].wait()
        part = pl.ds(c * piece, piece)
        for tile in range(order // 128):
            acts_f[tile, part, :] = acts_v[part, tile * 128 : (tile + 1) * 128].astype(F32)

    rs = {}
    greeted = False
    steps = list(range(n - 1, 0, -1))
    for slot in range(held):
        for step in steps:
            target = partner(me, step, n)[0]
            cross, packed, last = gram(target * held + slot)
            place = out_buf.at[step - 1, slot]
            place[:half, :] = cross.astype(BF16)
            place[half : 2 * half, :] = packed.astype(BF16)
            place[2 * half :, :] = jnp.broadcast_to(last, (16, half)).astype(BF16)
            if not greeted:
                pl.semaphore_wait(barrier, n - 1)
                greeted = True
            copy = pltpu.make_async_remote_copy(
                src_ref=place,
                dst_ref=in_buf.at[step - 1, slot],
                send_sem=rs_send.at[step - 1, slot],
                recv_sem=rs_recv.at[step - 1, slot],
                device_id={"rep": target},
                device_id_type=MESH,
            )
            copy.start()
            rs[step, slot] = copy
        cross, packed, last = gram(me * held + slot)
        own_f[slot, :half, :] = cross
        own_f[slot, half : 2 * half, :] = packed
        own_f[slot, 2 * half :, :] = jnp.broadcast_to(last, (8, half))

    loads[LOADS].wait()
    widen(grads_v, grads_f)
    loads[LOADS + 1].wait()

    eye = jnp.where(
        lax.broadcasted_iota(jnp.int32, (order, order), 0)
        == lax.broadcasted_iota(jnp.int32, (order, order), 1),
        1.0,
        0.0,
    ).astype(F32)

    ag = {}

    def ship(key, source, target, step, sem):
        copy = pltpu.make_async_remote_copy(
            src_ref=source,
            dst_ref=target,
            send_sem=ag_send.at[sem],
            recv_sem=ag_recv.at[sem],
            device_id={"rep": partner(me, step, n)[0]},
            device_id_type=MESH,
        )
        copy.start()
        ag[key] = copy

    def refresh_block(slot):
        total = own_f[slot]
        total_cross, total_packed, total_last = (
            total[:half],
            total[half : 2 * half],
            total[2 * half : 2 * half + 1],
        )
        for step in steps:
            rs[step, slot].wait_recv()
            came = in_buf[step - 1, slot].astype(F32)
            total_cross = total_cross + came[:half]
            total_packed = total_packed + came[half : 2 * half]
            total_last = total_last + came[2 * half : 2 * half + 1]
        scale = 1.0 / tokens_all
        flipped = total_packed.T
        first = jnp.where(upper, total_packed, flipped)
        second = jnp.where(
            on_diag,
            jnp.broadcast_to(total_last, (half, half)),
            jnp.where(upper, flipped, total_packed),
        )
        covariance = (
            jnp.concatenate(
                [
                    jnp.concatenate([first, total_cross], axis=1),
                    jnp.concatenate([total_cross.T, second], axis=1),
                ],
                axis=0,
            )
            * scale
        )
        cov_ref[slot] = covariance
        matrix = covariance + damping_ref[slot] * eye
        bound = jnp.max(jnp.sum(jnp.abs(matrix), axis=0, keepdims=True), axis=1, keepdims=True)
        inverse_bound = 1.0 / bound
        residual = eye - matrix * inverse_bound
        series = eye + residual
        power = split(residual)
        power = split(dot3(power, power))
        for iteration in range(2, ITERS):
            left = split(series)
            square = dot3(power, power)
            series = series + dot3(left, power)
            power = split(square)
        series = series + dot3(split(series), power)
        approx = (series * inverse_bound).astype(BF16)
        due = jnp.full((order, order), refresh_ref[slot], jnp.int32) != groups
        chosen = jnp.where(due, approx, old_v[slot])
        inv_ref[slot] = chosen
        gathered[0, slot] = chosen
        for step in steps:
            ship(
                (slot, step),
                gathered.at[0, slot],
                gathered.at[step, slot],
                step,
                slot * n + step,
            )

    def apply(step, slot):
        block = partner(me, step, n)[1] * held + slot
        result = jnp.dot(
            take(grads_f, block), gathered[step, slot], preferred_element_type=F32
        )
        for tile in range(order // 128):
            pre_f[tile, pl.ds(block, rows, stride=blocks), :] = result[
                :, tile * 128 : (tile + 1) * 128
            ]

    for slot in range(held):
        refresh_block(slot)
    for slot in range(held):
        apply(0, slot)
    for slot in range(held):
        for step in steps:
            ag[slot, step].wait_recv()
            apply(step, slot)
    for copy in rs.values():
        copy.wait_send()
    for copy in ag.values():
        copy.wait_send()


NEAR = (1, 2)
RSM = "half"
LATEM = ("relay", "relay")
GRADS_FIRST = False
RELAY_LATER = False
TOGETHER = True
EARLY = {"s2": ["d", "e"], "n1": ["dr", "er"]}


def square_kernel(
    held,
    groups,
    tokens_all,
    acts_hbm,
    refresh_hbm,
    damping_hbm,
    old_hbm,
    grads_hbm,
    cov_ref,
    inv_ref,
    pre_f,
    refresh_s,
    damping_s,
    acts_v,
    grads_v,
    old_v,
    acts_f,
    grads_f,
    grads_b,
    own_f,
    mid_f,
    sum_out,
    sum_in,
    early_own,
    early_in,
    late_own,
    late_in,
    load_sem,
    send_sem,
    recv_sem,
):
    n = 4
    me = lax.axis_index("rep")
    blocks = n * held
    order = inv_ref.shape[-1]
    half = order // 2
    rows = acts_v.shape[0] // blocks
    grad_rows = grads_v.shape[0] // blocks
    peer = [partner(me, step, n)[0] for step in range(n)]

    barrier = pltpu.get_barrier_semaphore()
    for step in NEAR:
        pl.semaphore_signal(
            barrier, inc=1, device_id={"rep": peer[step]}, device_id_type=MESH
        )

    piece = acts_v.shape[0] // LOADS
    acts_loads = [
        pltpu.make_async_copy(
            acts_hbm.at[pl.ds(c * piece, piece)],
            acts_v.at[pl.ds(c * piece, piece)],
            load_sem.at[4 + c],
        )
        for c in range(LOADS)
    ]
    old_load = pltpu.make_async_copy(old_hbm, old_v, load_sem.at[0])
    grads_load = pltpu.make_async_copy(grads_hbm, grads_v, load_sem.at[1])
    refresh_load = pltpu.make_async_copy(refresh_hbm, refresh_s, load_sem.at[2])
    damping_load = pltpu.make_async_copy(damping_hbm, damping_s, load_sem.at[3])
    for load in acts_loads + [old_load, refresh_load, damping_load, grads_load]:
        load.start()

    copies = {}

    def send(key, source, target, step):
        index = len(copies)
        copy = pltpu.make_async_remote_copy(
            src_ref=source,
            dst_ref=target,
            send_sem=send_sem.at[index],
            recv_sem=recv_sem.at[index],
            device_id={"rep": peer[step]},
            device_id_type=MESH,
        )
        copy.start()
        copies[key] = copy

    def arrived(*key):
        copies[key].wait_recv()

    row_id = lax.broadcasted_iota(jnp.int32, (half, half), 0)
    col_id = lax.broadcasted_iota(jnp.int32, (half, half), 1)
    upper = col_id >= row_id
    on_diag = col_id == row_id

    def widen(source, target, part):
        for tile in range(order // 128):
            target[tile, part, :] = source[part, tile * 128 : (tile + 1) * 128].astype(F32)

    def take(source, block, count):
        return jnp.concatenate(
            [
                source[tile, pl.ds(block, count, stride=blocks), :]
                for tile in range(order // 128)
            ],
            axis=1,
        ).astype(BF16)

    def diagonal(square):
        return jnp.sum(jnp.where(on_diag, square, 0.0), axis=0, keepdims=True)

    def gram(block):
        part = take(acts_f, block, rows)
        full = lax.dot_general(
            part, part, (((0,), (0,)), ((), ())), preferred_element_type=F32
        )
        low = full[half:, half:]
        return full[:half, half:], jnp.where(upper, full[:half, :half], low), diagonal(low)

    def keep(place, parts):
        cross, packed, last = parts
        place[:half, :] = cross.astype(place.dtype)
        place[half : 2 * half, :] = packed.astype(place.dtype)
        place[2 * half :, :] = jnp.broadcast_to(
            last, (place.shape[0] - 2 * half, half)
        ).astype(place.dtype)

    def parts_of(value):
        value = value.astype(F32)
        return value[:half], value[half : 2 * half], value[2 * half : 2 * half + 1]

    def add(*terms):
        return tuple(sum(entries[1:], entries[0]) for entries in zip(*terms))

    def axes(slot):
        return (1, 2) if slot % 2 == 0 else (2, 1)

    whole, first_half, last_half = pl.ds(0, half), pl.ds(0, half // 2), pl.ds(half // 2, half // 2)
    packed_whole = pl.ds(half, half)
    packed_first, packed_last = pl.ds(half, half // 2), pl.ds(half + half // 2, half // 2)

    def early_relay(kind, slot, first, last):
        arrived(kind, slot, 1)
        send((kind, slot, "y"), early_in.at[0, slot, first], early_in.at[2, slot, first], 2)
        arrived(kind, slot, 2)
        send((kind, slot, "x"), early_in.at[1, slot, last], early_in.at[2, slot, last], 1)

    def early_send(kind, slot):
        if kind == "d":
            source, place = old_hbm.at[slot, pl.ds(half, half), pl.ds(0, half)], whole
        else:
            source, place = early_own.at[slot], packed_whole
        for step in (1, 2):
            send((kind, slot, step), source, early_in.at[step - 1, slot, place], step)

    def early(point):
        for action in EARLY.get(point, ()):
            kind = action[0]
            slots = range(held) if len(action) == 1 or action[1] == "r" else [int(action[1])]
            for slot in slots:
                if action[-1] != "r":
                    early_send(kind, slot)
                elif kind == "d":
                    early_relay(kind, slot, first_half, last_half)
                else:
                    early_relay(kind, slot, packed_first, packed_last)

    pl.semaphore_wait(barrier, len(NEAR))
    early("start")

    for c in range(LOADS):
        acts_loads[c].wait()
        widen(acts_v, acts_f, pl.ds(c * piece, piece))

    def pack_old():
        old_load.wait()
        for slot in range(held):
            old = old_v[slot].astype(F32)
            early_own[slot] = jnp.where(upper, old[half:, half:], old[:half, :half]).astype(BF16)

    if RSM == "half":
        for stage in (0, 1):
            for slot in range(held):
                near, far = axes(slot)
                block = peer[3 if stage == 0 else near] * held + slot
                keep(sum_out.at[slot, stage], gram(block))
                send(("s", slot, stage), sum_out.at[slot, stage], sum_in.at[slot, stage], near)
        early("s1a")
        for slot in range(held):
            keep(mid_f.at[slot], gram(peer[axes(slot)[1]] * held + slot))
    else:
        for slot in range(held):
            for stage in (2, 0, 1):
                step = stage + 1
                keep(sum_out.at[slot, stage], gram(peer[step] * held + slot))
                send(("s", slot, stage), sum_out.at[slot, stage], sum_in.at[slot, stage], step)
        early("s1a")
    for slot in range(held):
        keep(own_f.at[slot], gram(me * held + slot))
    pack_old()
    early("s1")

    def spread_grads():
        grads_load.wait()
        widen(grads_v, grads_f, pl.ds(0, grads_v.shape[0]))
        for step in range(n):
            for slot in range(held):
                grads_b[step * held + slot] = take(grads_f, peer[step] * held + slot, grad_rows)

    if GRADS_FIRST:
        spread_grads()
    if RSM == "half":
        for slot in range(held):
            arrived("s", slot, 0)
            keep(sum_out.at[slot, 2], add(parts_of(mid_f[slot]), parts_of(sum_in[slot, 0])))
            send(("s", slot, 2), sum_out.at[slot, 2], sum_in.at[slot, 2], axes(slot)[1])
    early("s2")
    if not GRADS_FIRST:
        spread_grads()
    early("grads")
    one = functools.partial(jnp.dot, preferred_element_type=F32)
    eye = jnp.where(
        lax.broadcasted_iota(jnp.int32, (order, order), 0)
        == lax.broadcasted_iota(jnp.int32, (order, order), 1),
        1.0,
        0.0,
    ).astype(F32)
    refresh_load.wait()
    damping_load.wait()

    cut = (order + 16) // 32 * 16
    top, bottom = pl.ds(0, cut), pl.ds(cut, order + 16 - cut)

    def summed(slot):
        stages = (1, 2) if RSM == "half" else (0, 1, 2)
        for stage in stages:
            arrived("s", slot, stage)
        return add(parts_of(own_f[slot]), *(parts_of(sum_in[slot, stage]) for stage in stages))

    def assemble(slot, parts):
        cross, packed, last = (part * (1.0 / tokens_all) for part in parts)
        flipped = packed.T
        first = jnp.where(upper, packed, flipped)
        second = jnp.where(
            on_diag,
            jnp.broadcast_to(last, (half, half)),
            jnp.where(upper, flipped, packed),
        )
        covariance = jnp.concatenate(
            [
                jnp.concatenate([first, cross], axis=1),
                jnp.concatenate([cross.T, second], axis=1),
            ],
            axis=0,
        )
        cov_ref[slot] = covariance
        matrix = covariance + damping_s[slot] * eye
        bound = jnp.max(jnp.sum(jnp.abs(matrix), axis=0, keepdims=True), axis=1, keepdims=True)
        inverse_bound = 1.0 / bound
        return inverse_bound, eye - matrix * inverse_bound

    def newton(slots):
        bounds, residuals = zip(*(assemble(slot, summed(slot)) for slot in slots))
        many = range(len(slots))
        series = [eye + residual for residual in residuals]
        power = [split(residual) for residual in residuals]
        power = [split(dot3(item, item)) for item in power]
        for iteration in range(2, ITERS):
            last_one = iteration == ITERS - 1
            square = [one(item[0], item[0]) if last_one else dot3(item, item) for item in power]
            series = [series[i] + one(series[i].astype(BF16), power[i][0]) for i in many]
            power = [(item.astype(BF16),) if last_one else split(item) for item in square]
        for i in many:
            total = series[i] + one(series[i].astype(BF16), power[i][0])
            finish(slots[i], total * bounds[i])

    def finish(slot, approx):
        due = jnp.full((order, order), refresh_s[slot], jnp.int32) != groups
        chosen = jnp.where(due, approx.astype(BF16), old_v[slot])
        inv_ref[slot] = chosen
        chosen = chosen.astype(F32)
        low = chosen[half:, half:]
        late_own[slot, :half, :] = chosen[:half, half:].astype(BF16)
        late_own[slot, half:order, :] = jnp.where(upper, chosen[:half, :half], low).astype(BF16)
        due_row = jnp.where(jnp.full((8, half), refresh_s[slot], jnp.int32) != groups, 1.0, 0.0)
        late_own[slot, order:, :] = jnp.concatenate(
            [jnp.broadcast_to(diagonal(low), (8, half)), due_row], axis=0
        ).astype(BF16)

    def late_first(slot):
        if LATEM[slot] == "relay":
            send(("l", slot, 1, "top"), late_own.at[slot, top], late_in.at[0, slot, top], 1)
            send(("l", slot, 2, "bottom"), late_own.at[slot, bottom], late_in.at[1, slot, bottom], 2)
        else:
            send(("l", slot, 3), late_own.at[slot], late_in.at[2, slot], 3)

    def late_rest(slot):
        if LATEM[slot] == "relay":
            send(("l", slot, 1, "bottom"), late_own.at[slot, bottom], late_in.at[0, slot, bottom], 1)
            send(("l", slot, 2, "top"), late_own.at[slot, top], late_in.at[1, slot, top], 2)
        else:
            send(("l", slot, 1), late_own.at[slot], late_in.at[0, slot], 1)
            send(("l", slot, 2), late_own.at[slot], late_in.at[1, slot], 2)

    def late_relay(slot):
        if LATEM[slot] == "relay":
            arrived("l", slot, 1, "top")
            send(("l", slot, 3, "top"), late_in.at[0, slot, top], late_in.at[2, slot, top], 2)
            arrived("l", slot, 2, "bottom")
            send(("l", slot, 3, "bottom"), late_in.at[1, slot, bottom], late_in.at[2, slot, bottom], 1)

    def late_wait(step, slot):
        if LATEM[slot] == "direct":
            arrived("l", slot, step)
        elif step == 1:
            arrived("l", slot, 1, "bottom")
        elif step == 2:
            arrived("l", slot, 2, "top")
        else:
            arrived("l", slot, 3, "top")
            arrived("l", slot, 3, "bottom")

    def multiply(step, slot, inverse):
        block = peer[step] * held + slot
        result = jnp.dot(grads_b[step * held + slot], inverse, preferred_element_type=F32)
        for tile in range(order // 128):
            pre_f[tile, pl.ds(block, grad_rows, stride=blocks), :] = result[
                :, tile * 128 : (tile + 1) * 128
            ]

    def apply(step, slot):
        late = late_in[step - 1, slot].astype(F32)
        early = early_in[step - 1, slot].astype(F32)
        cross, packed = late[:half], late[half:order]
        last, flag = late[order : order + 1], late[order + 8 : order + 9]
        due = jnp.broadcast_to(flag, (half, half)) > 0.5
        other = jnp.where(
            due,
            jnp.where(on_diag, jnp.broadcast_to(last, (half, half)), packed.T),
            early[half:],
        )
        inverse = jnp.concatenate(
            [
                jnp.concatenate([jnp.where(upper, packed, other), cross], axis=1),
                jnp.concatenate(
                    [jnp.where(due, cross.T, early[:half]), jnp.where(upper, other, packed)], axis=1
                ),
            ],
            axis=0,
        ).astype(BF16)
        multiply(step, slot, inverse)

    if TOGETHER:
        newton(list(range(held)))
        for slot in range(held):
            late_first(slot)
        for slot in range(held):
            late_rest(slot)
        early("n1")
        for slot in range(held):
            multiply(0, slot, inv_ref[slot])
        for slot in range(held):
            late_relay(slot)
    else:
        for slot in range(held):
            newton([slot])
            late_first(slot)
            early("n%d" % slot)
            if slot > 0 and not RELAY_LATER:
                late_relay(slot - 1)
            late_rest(slot)
            early("m%d" % slot)
        if RELAY_LATER:
            for slot in range(held - 1):
                late_relay(slot)
        for slot in range(held):
            multiply(0, slot, inv_ref[slot])
        late_relay(held - 1)
    for kind in ("d", "e"):
        for slot in range(held):
            arrived(kind, slot, "x")
            arrived(kind, slot, "y")
    for slot in range(held):
        for step in (1, 2, 3):
            late_wait(step, slot)
            apply(step, slot)
    for copy in copies.values():
        copy.wait_send()


def deliver(cov_v, inv_v, wide, cov_hbm, inv_hbm, pre_hbm, narrow, sem):
    copies = [
        pltpu.make_async_copy(cov_v, cov_hbm, sem.at[0]),
        pltpu.make_async_copy(inv_v, inv_hbm, sem.at[1]),
    ]
    for copy in copies:
        copy.start()
    size = narrow.shape[0] // CHUNKS
    for chunk in range(CHUNKS):
        part = pl.ds(chunk * size, size)
        for tile in range(wide.shape[0]):
            narrow[part, tile * 128 : (tile + 1) * 128] = wide[tile, part, :].astype(BF16)
        copy = pltpu.make_async_copy(narrow.at[part], pre_hbm.at[part], sem.at[2 + chunk])
        copy.start()
        copies.append(copy)
    for copy in copies:
        copy.wait()


def local(acts, refresh, damping, old_inverse, grads):
    n = lax.axis_size("rep")
    groups = lax.axis_size("mp")
    rows, blocks, order = acts.shape
    grad_rows = grads.shape[0]
    held = refresh.shape[0]
    half = order // 2
    tiles = order // 128
    any_space = pl.BlockSpec(memory_space=pltpu.HBM)
    smem = pl.BlockSpec(memory_space=pltpu.SMEM)
    vmem = pl.BlockSpec(memory_space=pltpu.VMEM)
    wide_scratch = [
        pltpu.VMEM((rows * blocks, order), BF16),
        pltpu.VMEM((grad_rows * blocks, order), BF16),
        pltpu.VMEM((held, order, order), BF16),
        pltpu.VMEM((tiles, rows * blocks, 128), F32),
        pltpu.VMEM((tiles, grad_rows * blocks, 128), F32),
    ]
    if n == 4:
        body = functools.partial(square_kernel, held, groups, rows * n)
        scratch = (
            [pltpu.SMEM((held,), jnp.int32), pltpu.SMEM((held,), F32)]
            + wide_scratch
            + [
                pltpu.VMEM((blocks, grad_rows, order), BF16),
                pltpu.VMEM((held, order + 8, half), F32),
                pltpu.VMEM((held, order + 8, half), F32),
                pltpu.VMEM((held, 3, order + 16, half), BF16),
                pltpu.VMEM((held, 3, order + 16, half), BF16),
                pltpu.VMEM((held, half, half), BF16),
                pltpu.VMEM((3, held, order, half), BF16),
                pltpu.VMEM((held, order + 16, half), BF16),
                pltpu.VMEM((3, held, order + 16, half), BF16),
                pltpu.SemaphoreType.DMA((4 + LOADS,)),
                pltpu.SemaphoreType.DMA((17 * held,)),
                pltpu.SemaphoreType.DMA((17 * held,)),
            ]
        )
        small = any_space
    else:
        body = functools.partial(general_kernel, n, held, groups, rows * n)
        scratch = wide_scratch + [
            pltpu.VMEM((held, order + 8, half), F32),
            pltpu.VMEM((n - 1, held, order + 16, half), BF16),
            pltpu.VMEM((n - 1, held, order + 16, half), BF16),
            pltpu.VMEM((n, held, order, order), BF16),
            pltpu.SemaphoreType.DMA((3 + LOADS,)),
            pltpu.SemaphoreType.DMA((n - 1, held)),
            pltpu.SemaphoreType.DMA((n - 1, held)),
            pltpu.SemaphoreType.DMA((held * n,)),
            pltpu.SemaphoreType.DMA((held * n,)),
        ]
        small = smem
    need = sum(
        math.prod(item.shape) * jnp.dtype(item.dtype).itemsize
        for item in scratch
        if item.memory_space == pltpu.VMEM
    )
    covariance, new_inverse, wide = pl.pallas_call(
        body,
        out_shape=(
            pltpu.VMEM((held, order, order), F32),
            pltpu.VMEM((held, order, order), BF16),
            pltpu.VMEM((tiles, grad_rows * blocks, 128), F32),
        ),
        in_specs=[any_space, small, small, any_space, any_space],
        out_specs=(vmem, vmem, vmem),
        scratch_shapes=scratch,
        compiler_params=pltpu.CompilerParams(
            collective_id=0, has_side_effects=True, vmem_limit_bytes=need + (8 << 20)
        ),
    )(
        pltpu.with_memory_space_constraint(acts.reshape(rows * blocks, order), pltpu.HBM),
        pltpu.with_memory_space_constraint(refresh, pltpu.HBM),
        pltpu.with_memory_space_constraint(damping, pltpu.HBM),
        pltpu.with_memory_space_constraint(old_inverse, pltpu.HBM),
        pltpu.with_memory_space_constraint(grads.reshape(grad_rows * blocks, order), pltpu.HBM),
    )
    covariance, new_inverse, precond = pl.pallas_call(
        deliver,
        out_shape=(
            jax.ShapeDtypeStruct((held, order, order), F32),
            jax.ShapeDtypeStruct((held, order, order), BF16),
            jax.ShapeDtypeStruct((grad_rows * blocks, order), BF16),
        ),
        in_specs=[vmem] * 3,
        out_specs=(any_space,) * 3,
        scratch_shapes=[
            pltpu.VMEM((grad_rows * blocks, order), BF16),
            pltpu.SemaphoreType.DMA((2 + CHUNKS,)),
        ],
        compiler_params=pltpu.CompilerParams(
            vmem_limit_bytes=grad_rows * blocks * order * 2 + (2 << 20)
        ),
    )(covariance, new_inverse, wide)
    return covariance, new_inverse, precond.reshape(grad_rows, blocks, order)


def solution(mesh):
    return jax.shard_map(
        local,
        mesh=mesh,
        in_specs=(
            P("rep", "mp", None),
            P(("mp", "rep")),
            P(("mp", "rep")),
            P(("mp", "rep"), None, None),
            P("rep", "mp", None),
        ),
        out_specs=(
            P(("mp", "rep"), None, None),
            P(("mp", "rep"), None, None),
            P("rep", "mp", None),
        ),
        check_vma=False,
    )
```

```python
import functools
import math

import jax
import jax.numpy as jnp
from jax import lax
from jax.experimental import pallas as pl
from jax.experimental.pallas import tpu as pltpu
from jax.sharding import PartitionSpec as P

ITERS = 5
CHUNKS = 4
LOADS = 4
MESH = pl.DeviceIdType.MESH
F32 = jnp.float32
BF16 = jnp.bfloat16


def split(x):
    high = x.astype(BF16)
    return high, (x - high.astype(F32)).astype(BF16)


def dot3(lhs, rhs):
    lh, ll = lhs
    rh, rl = rhs
    mm = functools.partial(jnp.dot, preferred_element_type=F32)
    return mm(lh, rh) + (mm(lh, rl) + mm(ll, rh))


def partner(me, step, n):
    if n & (n - 1):
        return lax.rem(me + step, n), lax.rem(me + n - step, n)
    other = me
    bit = 1
    while bit < n:
        if step & bit:
            other = other + bit * (1 - 2 * lax.rem(me // bit, 2))
        bit *= 2
    return other, other


def general_kernel(
    n,
    held,
    groups,
    tokens_all,
    acts_hbm,
    refresh_ref,
    damping_ref,
    old_hbm,
    grads_hbm,
    cov_ref,
    inv_ref,
    pre_f,
    acts_v,
    grads_v,
    old_v,
    acts_f,
    grads_f,
    own_f,
    out_buf,
    in_buf,
    gathered,
    load_sem,
    rs_send,
    rs_recv,
    ag_send,
    ag_recv,
):
    me = lax.axis_index("rep")
    blocks = n * held
    order = inv_ref.shape[-1]
    half = order // 2
    rows = acts_v.shape[0] // blocks

    barrier = pltpu.get_barrier_semaphore()
    for step in range(1, n):
        pl.semaphore_signal(
            barrier, inc=1, device_id={"rep": partner(me, step, n)[0]}, device_id_type=MESH
        )

    piece = acts_v.shape[0] // LOADS
    loads = [
        pltpu.make_async_copy(acts_hbm.at[pl.ds(c * piece, piece)], acts_v.at[pl.ds(c * piece, piece)], load_sem.at[3 + c])
        for c in range(LOADS)
    ] + [
        pltpu.make_async_copy(grads_hbm, grads_v, load_sem.at[1]),
        pltpu.make_async_copy(old_hbm, old_v, load_sem.at[2]),
    ]
    for load in loads:
        load.start()

    row_id = lax.broadcasted_iota(jnp.int32, (half, half), 0)
    col_id = lax.broadcasted_iota(jnp.int32, (half, half), 1)
    upper = col_id >= row_id
    on_diag = col_id == row_id

    def widen(source, target):
        for tile in range(order // 128):
            target[tile] = source[:, tile * 128 : (tile + 1) * 128].astype(F32)

    def take(source, block):
        return jnp.concatenate(
            [
                source[tile, pl.ds(block, rows, stride=blocks), :]
                for tile in range(order // 128)
            ],
            axis=1,
        ).astype(BF16)

    def gram(block):
        part = take(acts_f, block)
        full = lax.dot_general(
            part, part, (((0,), (0,)), ((), ())), preferred_element_type=F32
        )
        low = full[half:, half:]
        last = jnp.sum(jnp.where(on_diag, low, 0.0), axis=0, keepdims=True)
        return full[:half, half:], jnp.where(upper, full[:half, :half], low), last

    for c in range(LOADS):
        loads[c].wait()
        part = pl.ds(c * piece, piece)
        for tile in range(order // 128):
            acts_f[tile, part, :] = acts_v[part, tile * 128 : (tile + 1) * 128].astype(F32)

    rs = {}
    greeted = False
    steps = list(range(n - 1, 0, -1))
    for slot in range(held):
        for step in steps:
            target = partner(me, step, n)[0]
            cross, packed, last = gram(target * held + slot)
            place = out_buf.at[step - 1, slot]
            place[:half, :] = cross.astype(BF16)
            place[half : 2 * half, :] = packed.astype(BF16)
            place[2 * half :, :] = jnp.broadcast_to(last, (16, half)).astype(BF16)
            if not greeted:
                pl.semaphore_wait(barrier, n - 1)
                greeted = True
            copy = pltpu.make_async_remote_copy(
                src_ref=place,
                dst_ref=in_buf.at[step - 1, slot],
                send_sem=rs_send.at[step - 1, slot],
                recv_sem=rs_recv.at[step - 1, slot],
                device_id={"rep": target},
                device_id_type=MESH,
            )
            copy.start()
            rs[step, slot] = copy
        cross, packed, last = gram(me * held + slot)
        own_f[slot, :half, :] = cross
        own_f[slot, half : 2 * half, :] = packed
        own_f[slot, 2 * half :, :] = jnp.broadcast_to(last, (8, half))

    loads[LOADS].wait()
    widen(grads_v, grads_f)
    loads[LOADS + 1].wait()

    eye = jnp.where(
        lax.broadcasted_iota(jnp.int32, (order, order), 0)
        == lax.broadcasted_iota(jnp.int32, (order, order), 1),
        1.0,
        0.0,
    ).astype(F32)

    ag = {}

    def ship(key, source, target, step, sem):
        copy = pltpu.make_async_remote_copy(
            src_ref=source,
            dst_ref=target,
            send_sem=ag_send.at[sem],
            recv_sem=ag_recv.at[sem],
            device_id={"rep": partner(me, step, n)[0]},
            device_id_type=MESH,
        )
        copy.start()
        ag[key] = copy

    def refresh_block(slot):
        total = own_f[slot]
        total_cross, total_packed, total_last = (
            total[:half],
            total[half : 2 * half],
            total[2 * half : 2 * half + 1],
        )
        for step in steps:
            rs[step, slot].wait_recv()
            came = in_buf[step - 1, slot].astype(F32)
            total_cross = total_cross + came[:half]
            total_packed = total_packed + came[half : 2 * half]
            total_last = total_last + came[2 * half : 2 * half + 1]
        scale = 1.0 / tokens_all
        flipped = total_packed.T
        first = jnp.where(upper, total_packed, flipped)
        second = jnp.where(
            on_diag,
            jnp.broadcast_to(total_last, (half, half)),
            jnp.where(upper, flipped, total_packed),
        )
        covariance = (
            jnp.concatenate(
                [
                    jnp.concatenate([first, total_cross], axis=1),
                    jnp.concatenate([total_cross.T, second], axis=1),
                ],
                axis=0,
            )
            * scale
        )
        cov_ref[slot] = covariance
        matrix = covariance + damping_ref[slot] * eye
        bound = jnp.max(jnp.sum(jnp.abs(matrix), axis=0, keepdims=True), axis=1, keepdims=True)
        inverse_bound = 1.0 / bound
        residual = eye - matrix * inverse_bound
        series = eye + residual
        power = split(residual)
        power = split(dot3(power, power))
        for iteration in range(2, ITERS):
            left = split(series)
            square = dot3(power, power)
            series = series + dot3(left, power)
            power = split(square)
        series = series + dot3(split(series), power)
        approx = (series * inverse_bound).astype(BF16)
        due = jnp.full((order, order), refresh_ref[slot], jnp.int32) != groups
        chosen = jnp.where(due, approx, old_v[slot])
        inv_ref[slot] = chosen
        gathered[0, slot] = chosen
        for step in steps:
            ship(
                (slot, step),
                gathered.at[0, slot],
                gathered.at[step, slot],
                step,
                slot * n + step,
            )

    def apply(step, slot):
        block = partner(me, step, n)[1] * held + slot
        result = jnp.dot(
            take(grads_f, block), gathered[step, slot], preferred_element_type=F32
        )
        for tile in range(order // 128):
            pre_f[tile, pl.ds(block, rows, stride=blocks), :] = result[
                :, tile * 128 : (tile + 1) * 128
            ]

    for slot in range(held):
        refresh_block(slot)
    for slot in range(held):
        apply(0, slot)
    for slot in range(held):
        for step in steps:
            ag[slot, step].wait_recv()
            apply(step, slot)
    for copy in rs.values():
        copy.wait_send()
    for copy in ag.values():
        copy.wait_send()


NEAR = (1, 2)
RSM = "half"
LATEM = ("relay", "relay")
GRADS_FIRST = False
RELAY_LATER = False
TOGETHER = True
EARLY = {"s2": ["d", "e"], "f1": ["dr", "er"]}
LOADS_LATER = True
TAIL = True
SQUARE = True
REST_LATER = False


def square_kernel(
    held,
    groups,
    tokens_all,
    acts_hbm,
    refresh_hbm,
    damping_hbm,
    old_hbm,
    grads_hbm,
    cov_ref,
    inv_ref,
    pre_f,
    refresh_s,
    damping_s,
    acts_v,
    grads_v,
    old_v,
    acts_f,
    grads_f,
    grads_b,
    own_f,
    mid_f,
    sum_out,
    sum_in,
    early_own,
    early_in,
    late_own,
    late_in,
    load_sem,
    send_sem,
    recv_sem,
):
    n = 4
    me = lax.axis_index("rep")
    blocks = n * held
    order = inv_ref.shape[-1]
    half = order // 2
    rows = acts_v.shape[0] // blocks
    grad_rows = grads_v.shape[0] // blocks
    peer = [partner(me, step, n)[0] for step in range(n)]

    barrier = pltpu.get_barrier_semaphore()
    for step in NEAR:
        pl.semaphore_signal(
            barrier, inc=1, device_id={"rep": peer[step]}, device_id_type=MESH
        )

    piece = acts_v.shape[0] // LOADS
    acts_loads = [
        pltpu.make_async_copy(
            acts_hbm.at[pl.ds(c * piece, piece)],
            acts_v.at[pl.ds(c * piece, piece)],
            load_sem.at[4 + c],
        )
        for c in range(LOADS)
    ]
    old_load = pltpu.make_async_copy(old_hbm, old_v, load_sem.at[0])
    grads_load = pltpu.make_async_copy(grads_hbm, grads_v, load_sem.at[1])
    refresh_load = pltpu.make_async_copy(refresh_hbm, refresh_s, load_sem.at[2])
    damping_load = pltpu.make_async_copy(damping_hbm, damping_s, load_sem.at[3])
    first_loads = acts_loads + ([] if LOADS_LATER else [old_load, refresh_load, damping_load, grads_load])
    for load in first_loads:
        load.start()

    copies = {}

    def send(key, source, target, step):
        index = len(copies)
        copy = pltpu.make_async_remote_copy(
            src_ref=source,
            dst_ref=target,
            send_sem=send_sem.at[index],
            recv_sem=recv_sem.at[index],
            device_id={"rep": peer[step]},
            device_id_type=MESH,
        )
        copy.start()
        copies[key] = copy

    def arrived(*key):
        copies[key].wait_recv()

    row_id = lax.broadcasted_iota(jnp.int32, (half, half), 0)
    col_id = lax.broadcasted_iota(jnp.int32, (half, half), 1)
    upper = col_id >= row_id
    on_diag = col_id == row_id

    def widen(source, target, part):
        for tile in range(order // 128):
            target[tile, part, :] = source[part, tile * 128 : (tile + 1) * 128].astype(F32)

    def take(source, block, count):
        return jnp.concatenate(
            [
                source[tile, pl.ds(block, count, stride=blocks), :]
                for tile in range(order // 128)
            ],
            axis=1,
        ).astype(BF16)

    def diagonal(square):
        return jnp.sum(jnp.where(on_diag, square, 0.0), axis=0, keepdims=True)

    def gram(block):
        part = take(acts_f, block, rows)
        full = lax.dot_general(
            part, part, (((0,), (0,)), ((), ())), preferred_element_type=F32
        )
        low = full[half:, half:]
        return full[:half, half:], jnp.where(upper, full[:half, :half], low), diagonal(low)

    def keep(place, parts):
        cross, packed, last = parts
        place[:half, :] = cross.astype(place.dtype)
        place[half : 2 * half, :] = packed.astype(place.dtype)
        place[2 * half :, :] = jnp.broadcast_to(
            last, (place.shape[0] - 2 * half, half)
        ).astype(place.dtype)

    def parts_of(value):
        value = value.astype(F32)
        return value[:half], value[half : 2 * half], value[2 * half : 2 * half + 1]

    def add(*terms):
        return tuple(sum(entries[1:], entries[0]) for entries in zip(*terms))

    def axes(slot):
        return (1, 2) if slot % 2 == 0 else (2, 1)

    whole, first_half, last_half = pl.ds(0, half), pl.ds(0, half // 2), pl.ds(half // 2, half // 2)
    packed_whole = pl.ds(half, half)
    packed_first, packed_last = pl.ds(half, half // 2), pl.ds(half + half // 2, half // 2)

    def early_relay(kind, slot, first, last):
        arrived(kind, slot, 1)
        send((kind, slot, "y"), early_in.at[0, slot, first], early_in.at[2, slot, first], 2)
        arrived(kind, slot, 2)
        send((kind, slot, "x"), early_in.at[1, slot, last], early_in.at[2, slot, last], 1)

    def early_send(kind, slot):
        if kind == "d":
            source, place = old_hbm.at[slot, pl.ds(half, half), pl.ds(0, half)], whole
        else:
            source, place = early_own.at[slot], packed_whole
        for step in (1, 2):
            send((kind, slot, step), source, early_in.at[step - 1, slot, place], step)

    def early(point):
        plan = EARLY.get(point, ())
        early_do(plan)

    def early_do(plan):
        for action in plan:
            kind = action[0]
            slots = range(held) if len(action) == 1 or action[1] == "r" else [int(action[1])]
            for slot in slots:
                if action[-1] != "r":
                    early_send(kind, slot)
                elif kind == "d":
                    early_relay(kind, slot, first_half, last_half)
                else:
                    early_relay(kind, slot, packed_first, packed_last)

    if EARLY.get("start"):
        pl.semaphore_wait(barrier, len(NEAR))
    early("start")

    for c in range(LOADS):
        acts_loads[c].wait()
        if LOADS_LATER and c == LOADS - 1:
            for load in (old_load, refresh_load, damping_load, grads_load):
                load.start()
        widen(acts_v, acts_f, pl.ds(c * piece, piece))

    def pack_old():
        old_load.wait()
        for slot in range(held):
            old = old_v[slot].astype(F32)
            early_own[slot] = jnp.where(upper, old[half:, half:], old[:half, :half]).astype(BF16)

    if RSM == "half":
        for stage in (0, 1):
            for slot in range(held):
                near, far = axes(slot)
                block = peer[3 if stage == 0 else near] * held + slot
                keep(sum_out.at[slot, stage], gram(block))
                if stage == 0 and slot == 0 and not EARLY.get("start"):
                    pl.semaphore_wait(barrier, len(NEAR))
                send(("s", slot, stage), sum_out.at[slot, stage], sum_in.at[slot, stage], near)
        early("s1a")
        for slot in range(held):
            keep(mid_f.at[slot], gram(peer[axes(slot)[1]] * held + slot))
    else:
        for slot in range(held):
            for stage in (2, 0, 1):
                step = stage + 1
                keep(sum_out.at[slot, stage], gram(peer[step] * held + slot))
                send(("s", slot, stage), sum_out.at[slot, stage], sum_in.at[slot, stage], step)
        early("s1a")
    for slot in range(held):
        keep(own_f.at[slot], gram(me * held + slot))
    pack_old()
    early("s1")

    def spread_grads():
        grads_load.wait()
        widen(grads_v, grads_f, pl.ds(0, grads_v.shape[0]))
        for step in range(n):
            for slot in range(held):
                grads_b[step * held + slot] = take(grads_f, peer[step] * held + slot, grad_rows)

    if GRADS_FIRST:
        spread_grads()
    if RSM == "half":
        for slot in range(held):
            arrived("s", slot, 0)
            keep(sum_out.at[slot, 2], add(parts_of(mid_f[slot]), parts_of(sum_in[slot, 0])))
            send(("s", slot, 2), sum_out.at[slot, 2], sum_in.at[slot, 2], axes(slot)[1])
    early("s2")
    if not GRADS_FIRST:
        spread_grads()
    early("grads")
    one = functools.partial(jnp.dot, preferred_element_type=F32)
    eye = jnp.where(
        lax.broadcasted_iota(jnp.int32, (order, order), 0)
        == lax.broadcasted_iota(jnp.int32, (order, order), 1),
        1.0,
        0.0,
    ).astype(F32)
    refresh_load.wait()
    damping_load.wait()

    cut = (order + 16) // 32 * 16
    top, bottom = pl.ds(0, cut), pl.ds(cut, order + 16 - cut)

    def summed(slot):
        stages = (1, 2) if RSM == "half" else (0, 1, 2)
        for stage in stages:
            arrived("s", slot, stage)
        return add(parts_of(own_f[slot]), *(parts_of(sum_in[slot, stage]) for stage in stages))

    def assemble(slot, parts):
        cross, packed, last = (part * (1.0 / tokens_all) for part in parts)
        flipped = packed.T
        first = jnp.where(upper, packed, flipped)
        second = jnp.where(
            on_diag,
            jnp.broadcast_to(last, (half, half)),
            jnp.where(upper, flipped, packed),
        )
        covariance = jnp.concatenate(
            [
                jnp.concatenate([first, cross], axis=1),
                jnp.concatenate([cross.T, second], axis=1),
            ],
            axis=0,
        )
        cov_ref[slot] = covariance
        matrix = covariance + damping_s[slot] * eye
        bound = jnp.max(jnp.sum(jnp.abs(matrix), axis=0, keepdims=True), axis=1, keepdims=True)
        inverse_bound = 1.0 / bound
        residual = eye - matrix * inverse_bound
        if not SQUARE:
            return inverse_bound, residual, split(dot3(split(residual), split(residual)))
        pair = split(matrix)
        square = dot3(pair, pair) * (inverse_bound * inverse_bound)
        return inverse_bound, residual, split(square + (residual - matrix * inverse_bound))

    def newton(slots):
        bounds, residuals, power = zip(*(assemble(slot, summed(slot)) for slot in slots))
        many = range(len(slots))
        series = [eye + residual for residual in residuals]
        for iteration in range(2, ITERS):
            last_one = iteration == ITERS - 1
            early("ns%d" % iteration)
            square = [one(item[0], item[0]) if last_one else dot3(item, item) for item in power]
            series = [series[i] + one(series[i].astype(BF16), power[i][0]) for i in many]
            power = [(item.astype(BF16),) if last_one else split(item) for item in square]
        for i in many:
            total = series[i] + one(series[i].astype(BF16), power[i][0])
            finish(slots[i], total * bounds[i])

    def finish(slot, approx):
        due = jnp.full((order, order), refresh_s[slot], jnp.int32) != groups
        chosen = jnp.where(due, approx.astype(BF16), old_v[slot])
        inv_ref[slot] = chosen
        chosen = chosen.astype(F32)
        low = chosen[half:, half:]
        late_own[slot, :half, :] = chosen[:half, half:].astype(BF16)
        late_own[slot, half:order, :] = jnp.where(upper, chosen[:half, :half], low).astype(BF16)
        due_row = jnp.where(jnp.full((8, half), refresh_s[slot], jnp.int32) != groups, 1.0, 0.0)
        late_own[slot, order:, :] = jnp.concatenate(
            [jnp.broadcast_to(diagonal(low), (8, half)), due_row], axis=0
        ).astype(BF16)

    def late_first(slot):
        if LATEM[slot] == "relay":
            send(("l", slot, 1, "top"), late_own.at[slot, top], late_in.at[0, slot, top], 1)
            send(("l", slot, 2, "bottom"), late_own.at[slot, bottom], late_in.at[1, slot, bottom], 2)
        else:
            send(("l", slot, 3), late_own.at[slot], late_in.at[2, slot], 3)

    def late_rest(slot):
        if LATEM[slot] == "relay":
            send(("l", slot, 1, "bottom"), late_own.at[slot, bottom], late_in.at[0, slot, bottom], 1)
            send(("l", slot, 2, "top"), late_own.at[slot, top], late_in.at[1, slot, top], 2)
        else:
            send(("l", slot, 1), late_own.at[slot], late_in.at[0, slot], 1)
            send(("l", slot, 2), late_own.at[slot], late_in.at[1, slot], 2)

    def late_relay(slot):
        if LATEM[slot] == "relay":
            arrived("l", slot, 1, "top")
            send(("l", slot, 3, "top"), late_in.at[0, slot, top], late_in.at[2, slot, top], 2)
            arrived("l", slot, 2, "bottom")
            send(("l", slot, 3, "bottom"), late_in.at[1, slot, bottom], late_in.at[2, slot, bottom], 1)

    def late_wait(step, slot):
        if LATEM[slot] == "direct":
            arrived("l", slot, step)
        elif step == 1:
            arrived("l", slot, 1, "bottom")
        elif step == 2:
            arrived("l", slot, 2, "top")
        else:
            arrived("l", slot, 3, "top")
            arrived("l", slot, 3, "bottom")

    def multiply(step, slot, inverse):
        block = peer[step] * held + slot
        result = jnp.dot(grads_b[step * held + slot], inverse, preferred_element_type=F32)
        for tile in range(order // 128):
            pre_f[tile, pl.ds(block, grad_rows, stride=blocks), :] = result[
                :, tile * 128 : (tile + 1) * 128
            ]

    def apply(step, slot):
        late = late_in[step - 1, slot].astype(F32)
        early = early_in[step - 1, slot].astype(F32)
        cross, packed = late[:half], late[half:order]
        last, flag = late[order : order + 1], late[order + 8 : order + 9]
        due = jnp.broadcast_to(flag, (half, half)) > 0.5
        other = jnp.where(
            due,
            jnp.where(on_diag, jnp.broadcast_to(last, (half, half)), packed.T),
            early[half:],
        )
        inverse = jnp.concatenate(
            [
                jnp.concatenate([jnp.where(upper, packed, other), cross], axis=1),
                jnp.concatenate(
                    [jnp.where(due, cross.T, early[:half]), jnp.where(upper, other, packed)], axis=1
                ),
            ],
            axis=0,
        ).astype(BF16)
        multiply(step, slot, inverse)

    if TOGETHER:
        newton(list(range(held)))
        for slot in range(held):
            late_first(slot)
        early("f1")
        for slot in range(held):
            late_rest(slot)
        early("n1")
        for slot in range(held):
            multiply(0, slot, inv_ref[slot])
        for slot in range(held):
            late_relay(slot)
    else:
        for slot in range(held):
            newton([slot])
            late_first(slot)
            early("n%d" % slot)
            if slot > 0 and not RELAY_LATER:
                late_relay(slot - 1)
            late_rest(slot)
            early("m%d" % slot)
        if RELAY_LATER:
            for slot in range(held - 1):
                late_relay(slot)
        for slot in range(held):
            multiply(0, slot, inv_ref[slot])
        late_relay(held - 1)
    for kind in ("d", "e"):
        for slot in range(held):
            arrived(kind, slot, "x")
            arrived(kind, slot, "y")
    order_of = [(step, slot) for slot in range(held) for step in (1, 2, 3)]
    if TAIL:
        order_of.sort(key=lambda item: item[0] == 3)
    for step, slot in order_of:
        late_wait(step, slot)
        apply(step, slot)
    for copy in copies.values():
        copy.wait_send()


def deliver(cov_v, inv_v, wide, cov_hbm, inv_hbm, pre_hbm, narrow, sem):
    copies = [
        pltpu.make_async_copy(cov_v, cov_hbm, sem.at[0]),
        pltpu.make_async_copy(inv_v, inv_hbm, sem.at[1]),
    ]
    for copy in copies:
        copy.start()
    size = narrow.shape[0] // CHUNKS
    for chunk in range(CHUNKS):
        part = pl.ds(chunk * size, size)
        for tile in range(wide.shape[0]):
            narrow[part, tile * 128 : (tile + 1) * 128] = wide[tile, part, :].astype(BF16)
        copy = pltpu.make_async_copy(narrow.at[part], pre_hbm.at[part], sem.at[2 + chunk])
        copy.start()
        copies.append(copy)
    for copy in copies:
        copy.wait()


def local(acts, refresh, damping, old_inverse, grads):
    n = lax.axis_size("rep")
    groups = lax.axis_size("mp")
    rows, blocks, order = acts.shape
    grad_rows = grads.shape[0]
    held = refresh.shape[0]
    half = order // 2
    tiles = order // 128
    any_space = pl.BlockSpec(memory_space=pltpu.HBM)
    smem = pl.BlockSpec(memory_space=pltpu.SMEM)
    vmem = pl.BlockSpec(memory_space=pltpu.VMEM)
    wide_scratch = [
        pltpu.VMEM((rows * blocks, order), BF16),
        pltpu.VMEM((grad_rows * blocks, order), BF16),
        pltpu.VMEM((held, order, order), BF16),
        pltpu.VMEM((tiles, rows * blocks, 128), F32),
        pltpu.VMEM((tiles, grad_rows * blocks, 128), F32),
    ]
    if n == 4:
        body = functools.partial(square_kernel, held, groups, rows * n)
        scratch = (
            [pltpu.SMEM((held,), jnp.int32), pltpu.SMEM((held,), F32)]
            + wide_scratch
            + [
                pltpu.VMEM((blocks, grad_rows, order), BF16),
                pltpu.VMEM((held, order + 8, half), F32),
                pltpu.VMEM((held, order + 8, half), F32),
                pltpu.VMEM((held, 3, order + 16, half), BF16),
                pltpu.VMEM((held, 3, order + 16, half), BF16),
                pltpu.VMEM((held, half, half), BF16),
                pltpu.VMEM((3, held, order, half), BF16),
                pltpu.VMEM((held, order + 16, half), BF16),
                pltpu.VMEM((3, held, order + 16, half), BF16),
                pltpu.SemaphoreType.DMA((4 + LOADS,)),
                pltpu.SemaphoreType.DMA((17 * held,)),
                pltpu.SemaphoreType.DMA((17 * held,)),
            ]
        )
        small = any_space
    else:
        body = functools.partial(general_kernel, n, held, groups, rows * n)
        scratch = wide_scratch + [
            pltpu.VMEM((held, order + 8, half), F32),
            pltpu.VMEM((n - 1, held, order + 16, half), BF16),
            pltpu.VMEM((n - 1, held, order + 16, half), BF16),
            pltpu.VMEM((n, held, order, order), BF16),
            pltpu.SemaphoreType.DMA((3 + LOADS,)),
            pltpu.SemaphoreType.DMA((n - 1, held)),
            pltpu.SemaphoreType.DMA((n - 1, held)),
            pltpu.SemaphoreType.DMA((held * n,)),
            pltpu.SemaphoreType.DMA((held * n,)),
        ]
        small = smem
    need = sum(
        math.prod(item.shape) * jnp.dtype(item.dtype).itemsize
        for item in scratch
        if item.memory_space == pltpu.VMEM
    )
    covariance, new_inverse, wide = pl.pallas_call(
        body,
        out_shape=(
            pltpu.VMEM((held, order, order), F32),
            pltpu.VMEM((held, order, order), BF16),
            pltpu.VMEM((tiles, grad_rows * blocks, 128), F32),
        ),
        in_specs=[any_space, small, small, any_space, any_space],
        out_specs=(vmem, vmem, vmem),
        scratch_shapes=scratch,
        compiler_params=pltpu.CompilerParams(
            collective_id=0, has_side_effects=True, vmem_limit_bytes=need + (8 << 20)
        ),
    )(
        pltpu.with_memory_space_constraint(acts.reshape(rows * blocks, order), pltpu.HBM),
        pltpu.with_memory_space_constraint(refresh, pltpu.HBM),
        pltpu.with_memory_space_constraint(damping, pltpu.HBM),
        pltpu.with_memory_space_constraint(old_inverse, pltpu.HBM),
        pltpu.with_memory_space_constraint(grads.reshape(grad_rows * blocks, order), pltpu.HBM),
    )
    covariance, new_inverse, precond = pl.pallas_call(
        deliver,
        out_shape=(
            jax.ShapeDtypeStruct((held, order, order), F32),
            jax.ShapeDtypeStruct((held, order, order), BF16),
            jax.ShapeDtypeStruct((grad_rows * blocks, order), BF16),
        ),
        in_specs=[vmem] * 3,
        out_specs=(any_space,) * 3,
        scratch_shapes=[
            pltpu.VMEM((grad_rows * blocks, order), BF16),
            pltpu.SemaphoreType.DMA((2 + CHUNKS,)),
        ],
        compiler_params=pltpu.CompilerParams(
            vmem_limit_bytes=grad_rows * blocks * order * 2 + (2 << 20)
        ),
    )(covariance, new_inverse, wide)
    return covariance, new_inverse, precond.reshape(grad_rows, blocks, order)


def solution(mesh):
    return jax.shard_map(
        local,
        mesh=mesh,
        in_specs=(
            P("rep", "mp", None),
            P(("mp", "rep")),
            P(("mp", "rep")),
            P(("mp", "rep"), None, None),
            P("rep", "mp", None),
        ),
        out_specs=(
            P(("mp", "rep"), None, None),
            P(("mp", "rep"), None, None),
            P("rep", "mp", None),
        ),
        check_vma=False,
    )
```

```python
import functools
import math

import jax
import jax.numpy as jnp
from jax import lax
from jax.experimental import pallas as pl
from jax.experimental.pallas import tpu as pltpu
from jax.sharding import PartitionSpec as P

ITERS = 5
CHUNKS = 4
LOADS = 4
MESH = pl.DeviceIdType.MESH
F32 = jnp.float32
BF16 = jnp.bfloat16


def split(x):
    high = x.astype(BF16)
    return high, (x - high.astype(F32)).astype(BF16)


def dot3(lhs, rhs):
    lh, ll = lhs
    rh, rl = rhs
    mm = functools.partial(jnp.dot, preferred_element_type=F32)
    return mm(lh, rh) + (mm(lh, rl) + mm(ll, rh))


def partner(me, step, n):
    if n & (n - 1):
        return lax.rem(me + step, n), lax.rem(me + n - step, n)
    other = me
    bit = 1
    while bit < n:
        if step & bit:
            other = other + bit * (1 - 2 * lax.rem(me // bit, 2))
        bit *= 2
    return other, other


def general_kernel(
    n,
    held,
    groups,
    tokens_all,
    acts_hbm,
    refresh_ref,
    damping_ref,
    old_hbm,
    grads_hbm,
    cov_ref,
    inv_ref,
    pre_f,
    acts_v,
    grads_v,
    old_v,
    acts_f,
    grads_f,
    own_f,
    out_buf,
    in_buf,
    gathered,
    load_sem,
    rs_send,
    rs_recv,
    ag_send,
    ag_recv,
):
    me = lax.axis_index("rep")
    blocks = n * held
    order = inv_ref.shape[-1]
    half = order // 2
    rows = acts_v.shape[0] // blocks

    barrier = pltpu.get_barrier_semaphore()
    for step in range(1, n):
        pl.semaphore_signal(
            barrier, inc=1, device_id={"rep": partner(me, step, n)[0]}, device_id_type=MESH
        )

    piece = acts_v.shape[0] // LOADS
    loads = [
        pltpu.make_async_copy(acts_hbm.at[pl.ds(c * piece, piece)], acts_v.at[pl.ds(c * piece, piece)], load_sem.at[3 + c])
        for c in range(LOADS)
    ] + [
        pltpu.make_async_copy(grads_hbm, grads_v, load_sem.at[1]),
        pltpu.make_async_copy(old_hbm, old_v, load_sem.at[2]),
    ]
    for load in loads:
        load.start()

    row_id = lax.broadcasted_iota(jnp.int32, (half, half), 0)
    col_id = lax.broadcasted_iota(jnp.int32, (half, half), 1)
    upper = col_id >= row_id
    on_diag = col_id == row_id

    def widen(source, target):
        for tile in range(order // 128):
            target[tile] = source[:, tile * 128 : (tile + 1) * 128].astype(F32)

    def take(source, block):
        return jnp.concatenate(
            [
                source[tile, pl.ds(block, rows, stride=blocks), :]
                for tile in range(order // 128)
            ],
            axis=1,
        ).astype(BF16)

    def gram(block):
        part = take(acts_f, block)
        full = lax.dot_general(
            part, part, (((0,), (0,)), ((), ())), preferred_element_type=F32
        )
        low = full[half:, half:]
        last = jnp.sum(jnp.where(on_diag, low, 0.0), axis=0, keepdims=True)
        return full[:half, half:], jnp.where(upper, full[:half, :half], low), last

    for c in range(LOADS):
        loads[c].wait()
        part = pl.ds(c * piece, piece)
        for tile in range(order // 128):
            acts_f[tile, part, :] = acts_v[part, tile * 128 : (tile + 1) * 128].astype(F32)

    rs = {}
    greeted = False
    steps = list(range(n - 1, 0, -1))
    for slot in range(held):
        for step in steps:
            target = partner(me, step, n)[0]
            cross, packed, last = gram(target * held + slot)
            place = out_buf.at[step - 1, slot]
            place[:half, :] = cross.astype(BF16)
            place[half : 2 * half, :] = packed.astype(BF16)
            place[2 * half :, :] = jnp.broadcast_to(last, (16, half)).astype(BF16)
            if not greeted:
                pl.semaphore_wait(barrier, n - 1)
                greeted = True
            copy = pltpu.make_async_remote_copy(
                src_ref=place,
                dst_ref=in_buf.at[step - 1, slot],
                send_sem=rs_send.at[step - 1, slot],
                recv_sem=rs_recv.at[step - 1, slot],
                device_id={"rep": target},
                device_id_type=MESH,
            )
            copy.start()
            rs[step, slot] = copy
        cross, packed, last = gram(me * held + slot)
        own_f[slot, :half, :] = cross
        own_f[slot, half : 2 * half, :] = packed
        own_f[slot, 2 * half :, :] = jnp.broadcast_to(last, (8, half))

    loads[LOADS].wait()
    widen(grads_v, grads_f)
    loads[LOADS + 1].wait()

    eye = jnp.where(
        lax.broadcasted_iota(jnp.int32, (order, order), 0)
        == lax.broadcasted_iota(jnp.int32, (order, order), 1),
        1.0,
        0.0,
    ).astype(F32)

    ag = {}

    def ship(key, source, target, step, sem):
        copy = pltpu.make_async_remote_copy(
            src_ref=source,
            dst_ref=target,
            send_sem=ag_send.at[sem],
            recv_sem=ag_recv.at[sem],
            device_id={"rep": partner(me, step, n)[0]},
            device_id_type=MESH,
        )
        copy.start()
        ag[key] = copy

    def refresh_block(slot):
        total = own_f[slot]
        total_cross, total_packed, total_last = (
            total[:half],
            total[half : 2 * half],
            total[2 * half : 2 * half + 1],
        )
        for step in steps:
            rs[step, slot].wait_recv()
            came = in_buf[step - 1, slot].astype(F32)
            total_cross = total_cross + came[:half]
            total_packed = total_packed + came[half : 2 * half]
            total_last = total_last + came[2 * half : 2 * half + 1]
        scale = 1.0 / tokens_all
        flipped = total_packed.T
        first = jnp.where(upper, total_packed, flipped)
        second = jnp.where(
            on_diag,
            jnp.broadcast_to(total_last, (half, half)),
            jnp.where(upper, flipped, total_packed),
        )
        covariance = (
            jnp.concatenate(
                [
                    jnp.concatenate([first, total_cross], axis=1),
                    jnp.concatenate([total_cross.T, second], axis=1),
                ],
                axis=0,
            )
            * scale
        )
        cov_ref[slot] = covariance
        matrix = covariance + damping_ref[slot] * eye
        bound = jnp.max(jnp.sum(jnp.abs(matrix), axis=0, keepdims=True), axis=1, keepdims=True)
        inverse_bound = 1.0 / bound
        residual = eye - matrix * inverse_bound
        series = eye + residual
        power = split(residual)
        power = split(dot3(power, power))
        for iteration in range(2, ITERS):
            left = split(series)
            square = dot3(power, power)
            series = series + dot3(left, power)
            power = split(square)
        series = series + dot3(split(series), power)
        approx = (series * inverse_bound).astype(BF16)
        due = jnp.full((order, order), refresh_ref[slot], jnp.int32) != groups
        chosen = jnp.where(due, approx, old_v[slot])
        inv_ref[slot] = chosen
        gathered[0, slot] = chosen
        for step in steps:
            ship(
                (slot, step),
                gathered.at[0, slot],
                gathered.at[step, slot],
                step,
                slot * n + step,
            )

    def apply(step, slot):
        block = partner(me, step, n)[1] * held + slot
        result = jnp.dot(
            take(grads_f, block), gathered[step, slot], preferred_element_type=F32
        )
        for tile in range(order // 128):
            pre_f[tile, pl.ds(block, rows, stride=blocks), :] = result[
                :, tile * 128 : (tile + 1) * 128
            ]

    for slot in range(held):
        refresh_block(slot)
    for slot in range(held):
        apply(0, slot)
    for slot in range(held):
        for step in steps:
            ag[slot, step].wait_recv()
            apply(step, slot)
    for copy in rs.values():
        copy.wait_send()
    for copy in ag.values():
        copy.wait_send()


def square_kernel(
    held,
    groups,
    tokens_all,
    acts_hbm,
    refresh_hbm,
    damping_hbm,
    old_hbm,
    grads_hbm,
    cov_ref,
    inv_ref,
    pre_f,
    refresh_s,
    damping_s,
    acts_v,
    grads_v,
    old_v,
    acts_f,
    grads_f,
    grads_b,
    own_f,
    mid_f,
    sum_out,
    sum_in,
    early_own,
    early_in,
    late_own,
    late_in,
    sent_bytes,
    load_sem,
    send_sem,
    recv_sem,
):
    n = 4
    me = lax.axis_index("rep")
    blocks = n * held
    order = inv_ref.shape[-1]
    half = order // 2
    rows = acts_v.shape[0] // blocks
    grad_rows = grads_v.shape[0] // blocks
    peer = [partner(me, step, n)[0] for step in range(n)]

    barrier = pltpu.get_barrier_semaphore()
    for step in (1, 2):
        pl.semaphore_signal(
            barrier, inc=1, device_id={"rep": peer[step]}, device_id_type=MESH
        )

    piece = acts_v.shape[0] // LOADS
    acts_loads = [
        pltpu.make_async_copy(
            acts_hbm.at[pl.ds(c * piece, piece)],
            acts_v.at[pl.ds(c * piece, piece)],
            load_sem.at[4 + c],
        )
        for c in range(LOADS)
    ]
    old_load = pltpu.make_async_copy(old_hbm, old_v, load_sem.at[0])
    grads_load = pltpu.make_async_copy(grads_hbm, grads_v, load_sem.at[1])
    refresh_load = pltpu.make_async_copy(refresh_hbm, refresh_s, load_sem.at[2])
    damping_load = pltpu.make_async_copy(damping_hbm, damping_s, load_sem.at[3])
    for load in acts_loads:
        load.start()

    landings = {}

    def copy_of(landing, source, target, step):
        return pltpu.make_async_remote_copy(
            src_ref=source,
            dst_ref=target,
            send_sem=send_sem.at[0],
            recv_sem=recv_sem.at[landings.setdefault(landing, len(landings))],
            device_id={"rep": peer[step]},
            device_id_type=MESH,
        )

    def send(landing, source, target, step):
        copy_of(landing, source, target, step).start()

    def arrived(landing, target):
        copy_of(landing, target, target, 1).wait_recv()

    row_id = lax.broadcasted_iota(jnp.int32, (half, half), 0)
    col_id = lax.broadcasted_iota(jnp.int32, (half, half), 1)
    upper = col_id >= row_id
    on_diag = col_id == row_id

    def widen(source, target, part):
        for tile in range(order // 128):
            target[tile, part, :] = source[part, tile * 128 : (tile + 1) * 128].astype(F32)

    def take(source, block, count):
        return jnp.concatenate(
            [
                source[tile, pl.ds(block, count, stride=blocks), :]
                for tile in range(order // 128)
            ],
            axis=1,
        ).astype(BF16)

    def diagonal(square):
        return jnp.sum(jnp.where(on_diag, square, 0.0), axis=0, keepdims=True)

    def gram(block):
        part = take(acts_f, block, rows)
        full = lax.dot_general(
            part, part, (((0,), (0,)), ((), ())), preferred_element_type=F32
        )
        low = full[half:, half:]
        return full[:half, half:], jnp.where(upper, full[:half, :half], low), diagonal(low)

    def keep(place, parts):
        cross, packed, last = parts
        place[:half, :] = cross.astype(place.dtype)
        place[half : 2 * half, :] = packed.astype(place.dtype)
        place[2 * half :, :] = jnp.broadcast_to(
            last, (place.shape[0] - 2 * half, half)
        ).astype(place.dtype)

    def parts_of(value):
        value = value.astype(F32)
        return value[:half], value[half : 2 * half], value[2 * half : 2 * half + 1]

    def add(*terms):
        return tuple(sum(entries[1:], entries[0]) for entries in zip(*terms))

    def axes(slot):
        return (1, 2) if slot % 2 == 0 else (2, 1)

    quarter = half // 2
    early_parts = {
        "d": (pl.ds(0, half), pl.ds(0, quarter), pl.ds(quarter, quarter)),
        "e": (pl.ds(half, half), pl.ds(half, quarter), pl.ds(half + quarter, quarter)),
    }

    def early_send():
        for kind in ("d", "e"):
            for slot in range(held):
                if kind == "d":
                    source = old_hbm.at[slot, pl.ds(half, half), pl.ds(0, half)]
                else:
                    source = early_own.at[slot]
                for step in (1, 2):
                    target = early_in.at[step - 1, slot, early_parts[kind][0]]
                    send(("early", step), source, target, step)

    def early_relay():
        for step in (1, 2):
            arrived(("early", step), early_in.at[step - 1])
            for kind in ("d", "e"):
                for slot in range(held):
                    part = early_parts[kind][step]
                    send(
                        ("early", 3),
                        early_in.at[step - 1, slot, part],
                        early_in.at[2, slot, part],
                        3 - step,
                    )

    for c in range(LOADS):
        acts_loads[c].wait()
        if c == LOADS - 1:
            for load in (old_load, refresh_load, damping_load, grads_load):
                load.start()
        widen(acts_v, acts_f, pl.ds(c * piece, piece))

    def pack_old():
        old_load.wait()
        for slot in range(held):
            old = old_v[slot].astype(F32)
            early_own[slot] = jnp.where(upper, old[half:, half:], old[:half, :half]).astype(BF16)

    for stage in (0, 1):
        for slot in range(held):
            near = axes(slot)[0]
            keep(sum_out.at[slot, stage], gram(peer[3 if stage == 0 else near] * held + slot))
            if stage == 0 and slot == 0:
                pl.semaphore_wait(barrier, 2)
            landing = ("pass", slot) if stage == 0 else "sums"
            send(landing, sum_out.at[slot, stage], sum_in.at[stage, slot], near)
    for slot in range(held):
        keep(mid_f.at[slot], gram(peer[axes(slot)[1]] * held + slot))
    for slot in range(held):
        keep(own_f.at[slot], gram(me * held + slot))
    old_load.wait()
    for slot in range(held):
        old = old_v[slot].astype(F32)
        early_own[slot] = jnp.where(upper, old[half:, half:], old[:half, :half]).astype(BF16)

    for slot in range(held):
        arrived(("pass", slot), sum_in.at[0, slot])
        keep(sum_out.at[slot, 2], add(parts_of(mid_f[slot]), parts_of(sum_in[0, slot])))
        send("sums", sum_out.at[slot, 2], sum_in.at[2, slot], axes(slot)[1])
    early_send()

    grads_load.wait()
    widen(grads_v, grads_f, pl.ds(0, grads_v.shape[0]))
    for step in range(n):
        for slot in range(held):
            grads_b[step * held + slot] = take(grads_f, peer[step] * held + slot, grad_rows)

    one = functools.partial(jnp.dot, preferred_element_type=F32)
    eye = jnp.where(
        lax.broadcasted_iota(jnp.int32, (order, order), 0)
        == lax.broadcasted_iota(jnp.int32, (order, order), 1),
        1.0,
        0.0,
    ).astype(F32)
    refresh_load.wait()
    damping_load.wait()

    cut = (order + 16) // 32 * 16
    top, bottom = pl.ds(0, cut), pl.ds(cut, order + 16 - cut)

    def summed(slot):
        return add(parts_of(own_f[slot]), parts_of(sum_in[1, slot]), parts_of(sum_in[2, slot]))

    def assemble(slot, parts):
        cross, packed, last = (part * (1.0 / tokens_all) for part in parts)
        flipped = packed.T
        first = jnp.where(upper, packed, flipped)
        second = jnp.where(
            on_diag,
            jnp.broadcast_to(last, (half, half)),
            jnp.where(upper, flipped, packed),
        )
        covariance = jnp.concatenate(
            [
                jnp.concatenate([first, cross], axis=1),
                jnp.concatenate([cross.T, second], axis=1),
            ],
            axis=0,
        )
        cov_ref[slot] = covariance
        matrix = covariance + damping_s[slot] * eye
        bound = jnp.max(jnp.sum(jnp.abs(matrix), axis=0, keepdims=True), axis=1, keepdims=True)
        inverse_bound = 1.0 / bound
        residual = eye - matrix * inverse_bound
        pair = split(matrix)
        square = dot3(pair, pair) * (inverse_bound * inverse_bound)
        return inverse_bound, residual, split(square + (residual - matrix * inverse_bound))

    def newton(slots):
        arrived("sums", sum_in.at[pl.ds(1, 2)])
        bounds, residuals, power = zip(*(assemble(slot, summed(slot)) for slot in slots))
        many = range(len(slots))
        series = [eye + residual for residual in residuals]
        for iteration in range(2, ITERS):
            last_one = iteration == ITERS - 1
            square = [one(item[0], item[0]) if last_one else dot3(item, item) for item in power]
            series = [series[i] + one(series[i].astype(BF16), power[i][0]) for i in many]
            power = [(item.astype(BF16),) if last_one else split(item) for item in square]
        for i in many:
            total = series[i] + one(series[i].astype(BF16), power[i][0])
            finish(slots[i], total * bounds[i])

    def finish(slot, approx):
        due = jnp.full((order, order), refresh_s[slot], jnp.int32) != groups
        chosen = jnp.where(due, approx.astype(BF16), old_v[slot])
        inv_ref[slot] = chosen
        chosen = chosen.astype(F32)
        low = chosen[half:, half:]
        late_own[slot, :half, :] = chosen[:half, half:].astype(BF16)
        late_own[slot, half:order, :] = jnp.where(upper, chosen[:half, :half], low).astype(BF16)
        due_row = jnp.where(jnp.full((8, half), refresh_s[slot], jnp.int32) != groups, 1.0, 0.0)
        late_own[slot, order:, :] = jnp.concatenate(
            [jnp.broadcast_to(diagonal(low), (8, half)), due_row], axis=0
        ).astype(BF16)

    def late_send(landing, slot, step, part):
        send(landing, late_own.at[slot, part], late_in.at[step - 1, slot, part], step)

    def late_relay(slot):
        for step, part in ((1, top), (2, bottom)):
            arrived(("first", slot, step), late_in.at[step - 1, slot, part])
            send(
                ("relay", slot),
                late_in.at[step - 1, slot, part],
                late_in.at[2, slot, part],
                3 - step,
            )

    def multiply(step, slot, inverse):
        block = peer[step] * held + slot
        result = jnp.dot(grads_b[step * held + slot], inverse, preferred_element_type=F32)
        for tile in range(order // 128):
            pre_f[tile, pl.ds(block, grad_rows, stride=blocks), :] = result[
                :, tile * 128 : (tile + 1) * 128
            ]

    def apply(step, slot):
        late = late_in[step - 1, slot].astype(F32)
        early = early_in[step - 1, slot].astype(F32)
        cross, packed = late[:half], late[half:order]
        last, flag = late[order : order + 1], late[order + 8 : order + 9]
        due = jnp.broadcast_to(flag, (half, half)) > 0.5
        other = jnp.where(
            due,
            jnp.where(on_diag, jnp.broadcast_to(last, (half, half)), packed.T),
            early[half:],
        )
        inverse = jnp.concatenate(
            [
                jnp.concatenate([jnp.where(upper, packed, other), cross], axis=1),
                jnp.concatenate(
                    [jnp.where(due, cross.T, early[:half]), jnp.where(upper, other, packed)], axis=1
                ),
            ],
            axis=0,
        ).astype(BF16)
        multiply(step, slot, inverse)

    newton(list(range(held)))
    for slot in range(held):
        late_send(("first", slot, 1), slot, 1, top)
        late_send(("first", slot, 2), slot, 2, bottom)
    early_relay()
    for slot in range(held):
        late_send(("rest", slot, 1), slot, 1, bottom)
        late_send(("rest", slot, 2), slot, 2, top)
    for slot in range(held):
        multiply(0, slot, inv_ref[slot])
    for slot in range(held):
        late_relay(slot)
    arrived(("early", 3), early_in.at[2])
    for slot in range(held):
        arrived(("rest", slot, 1), late_in.at[0, slot, bottom])
        apply(1, slot)
        arrived(("rest", slot, 2), late_in.at[1, slot, top])
        apply(2, slot)
    for slot in range(held):
        arrived(("relay", slot), late_in.at[2, slot])
        apply(3, slot)
    pltpu.make_async_copy(sent_bytes, sent_bytes, send_sem.at[0]).wait()


def deliver(cov_v, inv_v, wide, cov_hbm, inv_hbm, pre_hbm, narrow, sem):
    copies = [
        pltpu.make_async_copy(cov_v, cov_hbm, sem.at[0]),
        pltpu.make_async_copy(inv_v, inv_hbm, sem.at[1]),
    ]
    for copy in copies:
        copy.start()
    size = narrow.shape[0] // CHUNKS
    for chunk in range(CHUNKS):
        part = pl.ds(chunk * size, size)
        for tile in range(wide.shape[0]):
            narrow[part, tile * 128 : (tile + 1) * 128] = wide[tile, part, :].astype(BF16)
        copy = pltpu.make_async_copy(narrow.at[part], pre_hbm.at[part], sem.at[2 + chunk])
        copy.start()
        copies.append(copy)
    for copy in copies:
        copy.wait()


def local(acts, refresh, damping, old_inverse, grads):
    n = lax.axis_size("rep")
    groups = lax.axis_size("mp")
    rows, blocks, order = acts.shape
    grad_rows = grads.shape[0]
    held = refresh.shape[0]
    half = order // 2
    tiles = order // 128
    any_space = pl.BlockSpec(memory_space=pltpu.HBM)
    smem = pl.BlockSpec(memory_space=pltpu.SMEM)
    vmem = pl.BlockSpec(memory_space=pltpu.VMEM)
    wide_scratch = [
        pltpu.VMEM((rows * blocks, order), BF16),
        pltpu.VMEM((grad_rows * blocks, order), BF16),
        pltpu.VMEM((held, order, order), BF16),
        pltpu.VMEM((tiles, rows * blocks, 128), F32),
        pltpu.VMEM((tiles, grad_rows * blocks, 128), F32),
    ]
    if n == 4:
        body = functools.partial(square_kernel, held, groups, rows * n)
        scratch = (
            [pltpu.SMEM((held,), jnp.int32), pltpu.SMEM((held,), F32)]
            + wide_scratch
            + [
                pltpu.VMEM((blocks, grad_rows, order), BF16),
                pltpu.VMEM((held, order + 8, half), F32),
                pltpu.VMEM((held, order + 8, half), F32),
                pltpu.VMEM((held, 3, order + 16, half), BF16),
                pltpu.VMEM((3, held, order + 16, half), BF16),
                pltpu.VMEM((held, half, half), BF16),
                pltpu.VMEM((3, held, order, half), BF16),
                pltpu.VMEM((held, order + 16, half), BF16),
                pltpu.VMEM((3, held, order + 16, half), BF16),
                pltpu.VMEM((held * (6 * (order + 16) + 3 * order), half), BF16),
                pltpu.SemaphoreType.DMA((4 + LOADS,)),
                pltpu.SemaphoreType.DMA((1,)),
                pltpu.SemaphoreType.DMA((4 + 6 * held,)),
            ]
        )
        small = any_space
    else:
        body = functools.partial(general_kernel, n, held, groups, rows * n)
        scratch = wide_scratch + [
            pltpu.VMEM((held, order + 8, half), F32),
            pltpu.VMEM((n - 1, held, order + 16, half), BF16),
            pltpu.VMEM((n - 1, held, order + 16, half), BF16),
            pltpu.VMEM((n, held, order, order), BF16),
            pltpu.SemaphoreType.DMA((3 + LOADS,)),
            pltpu.SemaphoreType.DMA((n - 1, held)),
            pltpu.SemaphoreType.DMA((n - 1, held)),
            pltpu.SemaphoreType.DMA((held * n,)),
            pltpu.SemaphoreType.DMA((held * n,)),
        ]
        small = smem
    need = sum(
        math.prod(item.shape) * jnp.dtype(item.dtype).itemsize
        for item in scratch
        if item.memory_space == pltpu.VMEM
    )
    covariance, new_inverse, wide = pl.pallas_call(
        body,
        out_shape=(
            pltpu.VMEM((held, order, order), F32),
            pltpu.VMEM((held, order, order), BF16),
            pltpu.VMEM((tiles, grad_rows * blocks, 128), F32),
        ),
        in_specs=[any_space, small, small, any_space, any_space],
        out_specs=(vmem, vmem, vmem),
        scratch_shapes=scratch,
        compiler_params=pltpu.CompilerParams(
            collective_id=0, has_side_effects=True, vmem_limit_bytes=need + (8 << 20)
        ),
    )(
        pltpu.with_memory_space_constraint(acts.reshape(rows * blocks, order), pltpu.HBM),
        pltpu.with_memory_space_constraint(refresh, pltpu.HBM),
        pltpu.with_memory_space_constraint(damping, pltpu.HBM),
        pltpu.with_memory_space_constraint(old_inverse, pltpu.HBM),
        pltpu.with_memory_space_constraint(grads.reshape(grad_rows * blocks, order), pltpu.HBM),
    )
    covariance, new_inverse, precond = pl.pallas_call(
        deliver,
        out_shape=(
            jax.ShapeDtypeStruct((held, order, order), F32),
            jax.ShapeDtypeStruct((held, order, order), BF16),
            jax.ShapeDtypeStruct((grad_rows * blocks, order), BF16),
        ),
        in_specs=[vmem] * 3,
        out_specs=(any_space,) * 3,
        scratch_shapes=[
            pltpu.VMEM((grad_rows * blocks, order), BF16),
            pltpu.SemaphoreType.DMA((2 + CHUNKS,)),
        ],
        compiler_params=pltpu.CompilerParams(
            vmem_limit_bytes=grad_rows * blocks * order * 2 + (2 << 20)
        ),
    )(covariance, new_inverse, wide)
    return covariance, new_inverse, precond.reshape(grad_rows, blocks, order)


def solution(mesh):
    return jax.shard_map(
        local,
        mesh=mesh,
        in_specs=(
            P("rep", "mp", None),
            P(("mp", "rep")),
            P(("mp", "rep")),
            P(("mp", "rep"), None, None),
            P("rep", "mp", None),
        ),
        out_specs=(
            P(("mp", "rep"), None, None),
            P(("mp", "rep"), None, None),
            P("rep", "mp", None),
        ),
        check_vma=False,
    )
```

```python
import functools
import math

import jax
import jax.numpy as jnp
from jax import lax
from jax.experimental import pallas as pl
from jax.experimental.pallas import tpu as pltpu
from jax.sharding import PartitionSpec as P

ITERS = 5
CHUNKS = 2
LOADS = 2
MESH = pl.DeviceIdType.MESH
F32 = jnp.float32
BF16 = jnp.bfloat16


def split(x):
    high = x.astype(BF16)
    return high, (x - high.astype(F32)).astype(BF16)


def dot3(lhs, rhs):
    lh, ll = lhs
    rh, rl = rhs
    mm = functools.partial(jnp.dot, preferred_element_type=F32)
    return mm(lh, rh) + (mm(lh, rl) + mm(ll, rh))


def partner(me, step, n):
    if n & (n - 1):
        return lax.rem(me + step, n), lax.rem(me + n - step, n)
    other = me
    bit = 1
    while bit < n:
        if step & bit:
            other = other + bit * (1 - 2 * lax.rem(me // bit, 2))
        bit *= 2
    return other, other


def general_kernel(
    n,
    held,
    groups,
    tokens_all,
    acts_hbm,
    refresh_ref,
    damping_ref,
    old_hbm,
    grads_hbm,
    cov_ref,
    inv_ref,
    pre_f,
    acts_v,
    grads_v,
    old_v,
    acts_f,
    grads_f,
    own_f,
    out_buf,
    in_buf,
    gathered,
    load_sem,
    rs_send,
    rs_recv,
    ag_send,
    ag_recv,
):
    me = lax.axis_index("rep")
    blocks = n * held
    order = inv_ref.shape[-1]
    half = order // 2
    rows = acts_v.shape[0] // blocks

    barrier = pltpu.get_barrier_semaphore()
    for step in range(1, n):
        pl.semaphore_signal(
            barrier, inc=1, device_id={"rep": partner(me, step, n)[0]}, device_id_type=MESH
        )

    piece = acts_v.shape[0] // LOADS
    loads = [
        pltpu.make_async_copy(acts_hbm.at[pl.ds(c * piece, piece)], acts_v.at[pl.ds(c * piece, piece)], load_sem.at[3 + c])
        for c in range(LOADS)
    ] + [
        pltpu.make_async_copy(grads_hbm, grads_v, load_sem.at[1]),
        pltpu.make_async_copy(old_hbm, old_v, load_sem.at[2]),
    ]
    for load in loads:
        load.start()

    row_id = lax.broadcasted_iota(jnp.int32, (half, half), 0)
    col_id = lax.broadcasted_iota(jnp.int32, (half, half), 1)
    upper = col_id >= row_id
    on_diag = col_id == row_id

    def widen(source, target):
        for tile in range(order // 128):
            target[tile] = source[:, tile * 128 : (tile + 1) * 128].astype(F32)

    def take(source, block):
        return jnp.concatenate(
            [
                source[tile, pl.ds(block, rows, stride=blocks), :]
                for tile in range(order // 128)
            ],
            axis=1,
        ).astype(BF16)

    def gram(block):
        part = take(acts_f, block)
        full = lax.dot_general(
            part, part, (((0,), (0,)), ((), ())), preferred_element_type=F32
        )
        low = full[half:, half:]
        last = jnp.sum(jnp.where(on_diag, low, 0.0), axis=0, keepdims=True)
        return full[:half, half:], jnp.where(upper, full[:half, :half], low), last

    for c in range(LOADS):
        loads[c].wait()
        part = pl.ds(c * piece, piece)
        for tile in range(order // 128):
            acts_f[tile, part, :] = acts_v[part, tile * 128 : (tile + 1) * 128].astype(F32)

    rs = {}
    greeted = False
    steps = list(range(n - 1, 0, -1))
    for slot in range(held):
        for step in steps:
            target = partner(me, step, n)[0]
            cross, packed, last = gram(target * held + slot)
            place = out_buf.at[step - 1, slot]
            place[:half, :] = cross.astype(BF16)
            place[half : 2 * half, :] = packed.astype(BF16)
            place[2 * half :, :] = jnp.broadcast_to(last, (16, half)).astype(BF16)
            if not greeted:
                pl.semaphore_wait(barrier, n - 1)
                greeted = True
            copy = pltpu.make_async_remote_copy(
                src_ref=place,
                dst_ref=in_buf.at[step - 1, slot],
                send_sem=rs_send.at[step - 1, slot],
                recv_sem=rs_recv.at[step - 1, slot],
                device_id={"rep": target},
                device_id_type=MESH,
            )
            copy.start()
            rs[step, slot] = copy
        cross, packed, last = gram(me * held + slot)
        own_f[slot, :half, :] = cross
        own_f[slot, half : 2 * half, :] = packed
        own_f[slot, 2 * half :, :] = jnp.broadcast_to(last, (8, half))

    loads[LOADS].wait()
    widen(grads_v, grads_f)
    loads[LOADS + 1].wait()

    eye = jnp.where(
        lax.broadcasted_iota(jnp.int32, (order, order), 0)
        == lax.broadcasted_iota(jnp.int32, (order, order), 1),
        1.0,
        0.0,
    ).astype(F32)

    ag = {}

    def ship(key, source, target, step, sem):
        copy = pltpu.make_async_remote_copy(
            src_ref=source,
            dst_ref=target,
            send_sem=ag_send.at[sem],
            recv_sem=ag_recv.at[sem],
            device_id={"rep": partner(me, step, n)[0]},
            device_id_type=MESH,
        )
        copy.start()
        ag[key] = copy

    def refresh_block(slot):
        total = own_f[slot]
        total_cross, total_packed, total_last = (
            total[:half],
            total[half : 2 * half],
            total[2 * half : 2 * half + 1],
        )
        for step in steps:
            rs[step, slot].wait_recv()
            came = in_buf[step - 1, slot].astype(F32)
            total_cross = total_cross + came[:half]
            total_packed = total_packed + came[half : 2 * half]
            total_last = total_last + came[2 * half : 2 * half + 1]
        scale = 1.0 / tokens_all
        flipped = total_packed.T
        first = jnp.where(upper, total_packed, flipped)
        second = jnp.where(
            on_diag,
            jnp.broadcast_to(total_last, (half, half)),
            jnp.where(upper, flipped, total_packed),
        )
        covariance = (
            jnp.concatenate(
                [
                    jnp.concatenate([first, total_cross], axis=1),
                    jnp.concatenate([total_cross.T, second], axis=1),
                ],
                axis=0,
            )
            * scale
        )
        cov_ref[slot] = covariance
        matrix = covariance + damping_ref[slot] * eye
        bound = jnp.max(jnp.sum(jnp.abs(matrix), axis=0, keepdims=True), axis=1, keepdims=True)
        inverse_bound = 1.0 / bound
        residual = eye - matrix * inverse_bound
        series = eye + residual
        power = split(residual)
        power = split(dot3(power, power))
        for iteration in range(2, ITERS):
            left = split(series)
            square = dot3(power, power)
            series = series + dot3(left, power)
            power = split(square)
        series = series + dot3(split(series), power)
        approx = (series * inverse_bound).astype(BF16)
        due = jnp.full((order, order), refresh_ref[slot], jnp.int32) != groups
        chosen = jnp.where(due, approx, old_v[slot])
        inv_ref[slot] = chosen
        gathered[0, slot] = chosen
        for step in steps:
            ship(
                (slot, step),
                gathered.at[0, slot],
                gathered.at[step, slot],
                step,
                slot * n + step,
            )

    def apply(step, slot):
        block = partner(me, step, n)[1] * held + slot
        result = jnp.dot(
            take(grads_f, block), gathered[step, slot], preferred_element_type=F32
        )
        for tile in range(order // 128):
            pre_f[tile, pl.ds(block, rows, stride=blocks), :] = result[
                :, tile * 128 : (tile + 1) * 128
            ]

    for slot in range(held):
        refresh_block(slot)
    for slot in range(held):
        apply(0, slot)
    for slot in range(held):
        for step in steps:
            ag[slot, step].wait_recv()
            apply(step, slot)
    for copy in rs.values():
        copy.wait_send()
    for copy in ag.values():
        copy.wait_send()


def square_kernel(
    held,
    groups,
    tokens_all,
    acts_hbm,
    refresh_hbm,
    damping_hbm,
    old_hbm,
    grads_hbm,
    cov_ref,
    inv_ref,
    pre_f,
    refresh_s,
    damping_s,
    acts_v,
    grads_v,
    old_v,
    acts_f,
    grads_f,
    grads_b,
    own_f,
    mid_f,
    sum_out,
    sum_in,
    early_own,
    early_in,
    late_own,
    late_in,
    sent_bytes,
    load_sem,
    send_sem,
    recv_sem,
):
    n = 4
    me = lax.axis_index("rep")
    blocks = n * held
    order = inv_ref.shape[-1]
    half = order // 2
    rows = acts_v.shape[0] // blocks
    grad_rows = grads_v.shape[0] // blocks
    peer = [partner(me, step, n)[0] for step in range(n)]

    barrier = pltpu.get_barrier_semaphore()
    for step in (1, 2):
        pl.semaphore_signal(
            barrier, inc=1, device_id={"rep": peer[step]}, device_id_type=MESH
        )

    piece = acts_v.shape[0] // LOADS
    acts_loads = [
        pltpu.make_async_copy(
            acts_hbm.at[pl.ds(c * piece, piece)],
            acts_v.at[pl.ds(c * piece, piece)],
            load_sem.at[4 + c],
        )
        for c in range(LOADS)
    ]
    old_load = pltpu.make_async_copy(old_hbm, old_v, load_sem.at[0])
    grads_load = pltpu.make_async_copy(grads_hbm, grads_v, load_sem.at[1])
    refresh_load = pltpu.make_async_copy(refresh_hbm, refresh_s, load_sem.at[2])
    damping_load = pltpu.make_async_copy(damping_hbm, damping_s, load_sem.at[3])
    for load in acts_loads:
        load.start()

    landings = {}

    def copy_of(landing, source, target, step):
        return pltpu.make_async_remote_copy(
            src_ref=source,
            dst_ref=target,
            send_sem=send_sem.at[0],
            recv_sem=recv_sem.at[landings.setdefault(landing, len(landings))],
            device_id={"rep": peer[step]},
            device_id_type=MESH,
        )

    def send(landing, source, target, step):
        copy_of(landing, source, target, step).start()

    def arrived(landing, target):
        copy_of(landing, target, target, 1).wait_recv()

    row_id = lax.broadcasted_iota(jnp.int32, (half, half), 0)
    col_id = lax.broadcasted_iota(jnp.int32, (half, half), 1)
    upper = col_id >= row_id
    on_diag = col_id == row_id

    def widen(source, target, part):
        for tile in range(order // 128):
            target[tile, part, :] = source[part, tile * 128 : (tile + 1) * 128].astype(F32)

    def take(source, block, count):
        return jnp.concatenate(
            [
                source[tile, pl.ds(block, count, stride=blocks), :]
                for tile in range(order // 128)
            ],
            axis=1,
        ).astype(BF16)

    def diagonal(square):
        return jnp.sum(jnp.where(on_diag, square, 0.0), axis=0, keepdims=True)

    def gram(block):
        part = take(acts_f, block, rows)
        full = lax.dot_general(
            part, part, (((0,), (0,)), ((), ())), preferred_element_type=F32
        )
        low = full[half:, half:]
        return full[:half, half:], jnp.where(upper, full[:half, :half], low), diagonal(low)

    def keep(place, parts):
        cross, packed, last = parts
        place[:half, :] = cross.astype(place.dtype)
        place[half : 2 * half, :] = packed.astype(place.dtype)
        place[2 * half :, :] = jnp.broadcast_to(
            last, (place.shape[0] - 2 * half, half)
        ).astype(place.dtype)

    def parts_of(value):
        value = value.astype(F32)
        return value[:half], value[half : 2 * half], value[2 * half : 2 * half + 1]

    def add(*terms):
        return tuple(sum(entries[1:], entries[0]) for entries in zip(*terms))

    def axes(slot):
        return (1, 2) if slot % 2 == 0 else (2, 1)

    quarter = half // 2
    early_parts = {
        "d": (pl.ds(0, half), pl.ds(0, quarter), pl.ds(quarter, quarter)),
        "e": (pl.ds(half, half), pl.ds(half, quarter), pl.ds(half + quarter, quarter)),
    }

    def early_send():
        for kind in ("d", "e"):
            for step in (1, 2):
                source = old_hbm.at[:, pl.ds(half, half), pl.ds(0, half)] if kind == "d" else early_own
                send(("early", step), source, early_in.at[step - 1, :, early_parts[kind][0]], step)

    def early_relay():
        for step in (1, 2):
            arrived(("early", step), early_in.at[step - 1])
            for kind in ("d", "e"):
                part = early_parts[kind][step]
                send(
                    ("early", 3),
                    early_in.at[step - 1, :, part],
                    early_in.at[2, :, part],
                    3 - step,
                )

    for c in range(LOADS):
        acts_loads[c].wait()
        if c == LOADS - 1:
            for load in (old_load, refresh_load, damping_load, grads_load):
                load.start()
        widen(acts_v, acts_f, pl.ds(c * piece, piece))

    def pack_old():
        old_load.wait()
        for slot in range(held):
            old = old_v[slot].astype(F32)
            early_own[slot] = jnp.where(upper, old[half:, half:], old[:half, :half]).astype(BF16)

    for stage in (0, 1):
        for slot in range(held):
            near = axes(slot)[0]
            keep(sum_out.at[slot, stage], gram(peer[3 if stage == 0 else near] * held + slot))
            if stage == 0 and slot == 0:
                pl.semaphore_wait(barrier, 2)
            landing = ("pass", slot) if stage == 0 else "sums"
            send(landing, sum_out.at[slot, stage], sum_in.at[stage, slot], near)
    for slot in range(held):
        keep(mid_f.at[slot], gram(peer[axes(slot)[1]] * held + slot))
    for slot in range(held):
        keep(own_f.at[slot], gram(me * held + slot))
    old_load.wait()
    for slot in range(held):
        old = old_v[slot].astype(F32)
        early_own[slot] = jnp.where(upper, old[half:, half:], old[:half, :half]).astype(BF16)

    for slot in range(held):
        arrived(("pass", slot), sum_in.at[0, slot])
        keep(sum_out.at[slot, 2], add(parts_of(mid_f[slot]), parts_of(sum_in[0, slot])))
        send("sums", sum_out.at[slot, 2], sum_in.at[2, slot], axes(slot)[1])
    early_send()

    grads_load.wait()
    widen(grads_v, grads_f, pl.ds(0, grads_v.shape[0]))
    for step in range(n):
        for slot in range(held):
            grads_b[step * held + slot] = take(grads_f, peer[step] * held + slot, grad_rows)

    one = functools.partial(jnp.dot, preferred_element_type=F32)
    eye = jnp.where(
        lax.broadcasted_iota(jnp.int32, (order, order), 0)
        == lax.broadcasted_iota(jnp.int32, (order, order), 1),
        1.0,
        0.0,
    ).astype(F32)
    refresh_load.wait()
    damping_load.wait()

    cut = (order + 16) // 32 * 16
    top, bottom = pl.ds(0, cut), pl.ds(cut, order + 16 - cut)

    def summed(slot):
        return add(parts_of(own_f[slot]), parts_of(sum_in[1, slot]), parts_of(sum_in[2, slot]))

    def assemble(slot, parts):
        cross, packed, last = (part * (1.0 / tokens_all) for part in parts)
        flipped = packed.T
        first = jnp.where(upper, packed, flipped)
        second = jnp.where(
            on_diag,
            jnp.broadcast_to(last, (half, half)),
            jnp.where(upper, flipped, packed),
        )
        covariance = jnp.concatenate(
            [
                jnp.concatenate([first, cross], axis=1),
                jnp.concatenate([cross.T, second], axis=1),
            ],
            axis=0,
        )
        cov_ref[slot] = covariance
        matrix = covariance + damping_s[slot] * eye
        bound = jnp.max(jnp.sum(jnp.abs(matrix), axis=0, keepdims=True), axis=1, keepdims=True)
        inverse_bound = 1.0 / bound
        residual = eye - matrix * inverse_bound
        pair = split(matrix)
        square = dot3(pair, pair) * (inverse_bound * inverse_bound)
        return inverse_bound, residual, split(square + (residual - matrix * inverse_bound))

    def newton(slots):
        arrived("sums", sum_in.at[pl.ds(1, 2)])
        bounds, residuals, power = zip(*(assemble(slot, summed(slot)) for slot in slots))
        many = range(len(slots))
        series = [eye + residual for residual in residuals]
        for iteration in range(2, ITERS):
            last_one = iteration == ITERS - 1
            square = [one(item[0], item[0]) if last_one else dot3(item, item) for item in power]
            series = [series[i] + one(series[i].astype(BF16), power[i][0]) for i in many]
            power = [(item.astype(BF16),) if last_one else split(item) for item in square]
        for i in many:
            total = series[i] + one(series[i].astype(BF16), power[i][0])
            finish(slots[i], total * bounds[i])
            late_first(slots[i])

    def finish(slot, approx):
        due = jnp.full((order, order), refresh_s[slot], jnp.int32) != groups
        chosen = jnp.where(due, approx.astype(BF16), old_v[slot])
        inv_ref[slot] = chosen
        chosen = chosen.astype(F32)
        low = chosen[half:, half:]
        late_own[slot, :half, :] = chosen[:half, half:].astype(BF16)
        late_own[slot, half:order, :] = jnp.where(upper, chosen[:half, :half], low).astype(BF16)
        due_row = jnp.where(jnp.full((8, half), refresh_s[slot], jnp.int32) != groups, 1.0, 0.0)
        late_own[slot, order:, :] = jnp.concatenate(
            [jnp.broadcast_to(diagonal(low), (8, half)), due_row], axis=0
        ).astype(BF16)

    def late_send(landing, slot, step, part):
        send(landing, late_own.at[slot, part], late_in.at[step - 1, slot, part], step)

    def late_first(slot):
        late_send(("first", slot, 1), slot, 1, top)
        late_send(("first", slot, 2), slot, 2, bottom)

    def late_relay(slot):
        for step, part in ((1, top), (2, bottom)):
            arrived(("first", slot, step), late_in.at[step - 1, slot, part])
            send(
                ("relay", slot),
                late_in.at[step - 1, slot, part],
                late_in.at[2, slot, part],
                3 - step,
            )

    def multiply(step, slot, inverse):
        block = peer[step] * held + slot
        result = jnp.dot(grads_b[step * held + slot], inverse, preferred_element_type=F32)
        for tile in range(order // 128):
            pre_f[tile, pl.ds(block, grad_rows, stride=blocks), :] = result[
                :, tile * 128 : (tile + 1) * 128
            ]

    def apply(step, slot):
        late = late_in[step - 1, slot].astype(F32)
        early = early_in[step - 1, slot].astype(F32)
        cross, packed = late[:half], late[half:order]
        last, flag = late[order : order + 1], late[order + 8 : order + 9]
        due = jnp.broadcast_to(flag, (half, half)) > 0.5
        other = jnp.where(
            due,
            jnp.where(on_diag, jnp.broadcast_to(last, (half, half)), packed.T),
            early[half:],
        )
        inverse = jnp.concatenate(
            [
                jnp.concatenate([jnp.where(upper, packed, other), cross], axis=1),
                jnp.concatenate(
                    [jnp.where(due, cross.T, early[:half]), jnp.where(upper, other, packed)], axis=1
                ),
            ],
            axis=0,
        ).astype(BF16)
        multiply(step, slot, inverse)

    newton(list(range(held)))
    early_relay()
    for step, part in ((1, bottom), (2, top)):
        send(("rest", step), late_own.at[:, part], late_in.at[step - 1, :, part], step)
    for slot in range(held):
        multiply(0, slot, inv_ref[slot])
    for slot in range(held):
        late_relay(slot)
    arrived(("early", 3), early_in.at[2])
    for step, part in ((1, bottom), (2, top)):
        arrived(("rest", step), late_in.at[step - 1, :, part])
        for slot in range(held):
            apply(step, slot)
    for slot in range(held):
        arrived(("relay", slot), late_in.at[2, slot])
        apply(3, slot)
    pltpu.make_async_copy(sent_bytes, sent_bytes, send_sem.at[0]).wait()


def deliver(cov_v, inv_v, wide, cov_hbm, inv_hbm, pre_hbm, narrow, sem):
    copies = [
        pltpu.make_async_copy(cov_v, cov_hbm, sem.at[0]),
        pltpu.make_async_copy(inv_v, inv_hbm, sem.at[1]),
    ]
    for copy in copies:
        copy.start()
    size = narrow.shape[0] // CHUNKS
    for chunk in range(CHUNKS):
        part = pl.ds(chunk * size, size)
        for tile in range(wide.shape[0]):
            narrow[part, tile * 128 : (tile + 1) * 128] = wide[tile, part, :].astype(BF16)
        copy = pltpu.make_async_copy(narrow.at[part], pre_hbm.at[part], sem.at[2 + chunk])
        copy.start()
        copies.append(copy)
    for copy in copies:
        copy.wait()


def local(acts, refresh, damping, old_inverse, grads):
    n = lax.axis_size("rep")
    groups = lax.axis_size("mp")
    rows, blocks, order = acts.shape
    grad_rows = grads.shape[0]
    held = refresh.shape[0]
    half = order // 2
    tiles = order // 128
    any_space = pl.BlockSpec(memory_space=pltpu.HBM)
    smem = pl.BlockSpec(memory_space=pltpu.SMEM)
    vmem = pl.BlockSpec(memory_space=pltpu.VMEM)
    wide_scratch = [
        pltpu.VMEM((rows * blocks, order), BF16),
        pltpu.VMEM((grad_rows * blocks, order), BF16),
        pltpu.VMEM((held, order, order), BF16),
        pltpu.VMEM((tiles, rows * blocks, 128), F32),
        pltpu.VMEM((tiles, grad_rows * blocks, 128), F32),
    ]
    if n == 4:
        body = functools.partial(square_kernel, held, groups, rows * n)
        scratch = (
            [pltpu.SMEM((held,), jnp.int32), pltpu.SMEM((held,), F32)]
            + wide_scratch
            + [
                pltpu.VMEM((blocks, grad_rows, order), BF16),
                pltpu.VMEM((held, order + 8, half), F32),
                pltpu.VMEM((held, order + 8, half), F32),
                pltpu.VMEM((held, 3, order + 16, half), BF16),
                pltpu.VMEM((3, held, order + 16, half), BF16),
                pltpu.VMEM((held, half, half), BF16),
                pltpu.VMEM((3, held, order, half), BF16),
                pltpu.VMEM((held, order + 16, half), BF16),
                pltpu.VMEM((3, held, order + 16, half), BF16),
                pltpu.VMEM((held * (6 * (order + 16) + 3 * order), half), BF16),
                pltpu.SemaphoreType.DMA((4 + LOADS,)),
                pltpu.SemaphoreType.DMA((1,)),
                pltpu.SemaphoreType.DMA((6 + 4 * held,)),
            ]
        )
        small = any_space
    else:
        body = functools.partial(general_kernel, n, held, groups, rows * n)
        scratch = wide_scratch + [
            pltpu.VMEM((held, order + 8, half), F32),
            pltpu.VMEM((n - 1, held, order + 16, half), BF16),
            pltpu.VMEM((n - 1, held, order + 16, half), BF16),
            pltpu.VMEM((n, held, order, order), BF16),
            pltpu.SemaphoreType.DMA((3 + LOADS,)),
            pltpu.SemaphoreType.DMA((n - 1, held)),
            pltpu.SemaphoreType.DMA((n - 1, held)),
            pltpu.SemaphoreType.DMA((held * n,)),
            pltpu.SemaphoreType.DMA((held * n,)),
        ]
        small = smem
    need = sum(
        math.prod(item.shape) * jnp.dtype(item.dtype).itemsize
        for item in scratch
        if item.memory_space == pltpu.VMEM
    )
    covariance, new_inverse, wide = pl.pallas_call(
        body,
        out_shape=(
            pltpu.VMEM((held, order, order), F32),
            pltpu.VMEM((held, order, order), BF16),
            pltpu.VMEM((tiles, grad_rows * blocks, 128), F32),
        ),
        in_specs=[any_space, small, small, any_space, any_space],
        out_specs=(vmem, vmem, vmem),
        scratch_shapes=scratch,
        compiler_params=pltpu.CompilerParams(
            collective_id=0, has_side_effects=True, vmem_limit_bytes=need + (8 << 20)
        ),
    )(
        pltpu.with_memory_space_constraint(acts.reshape(rows * blocks, order), pltpu.HBM),
        pltpu.with_memory_space_constraint(refresh, pltpu.HBM),
        pltpu.with_memory_space_constraint(damping, pltpu.HBM),
        pltpu.with_memory_space_constraint(old_inverse, pltpu.HBM),
        pltpu.with_memory_space_constraint(grads.reshape(grad_rows * blocks, order), pltpu.HBM),
    )
    covariance, new_inverse, precond = pl.pallas_call(
        deliver,
        out_shape=(
            jax.ShapeDtypeStruct((held, order, order), F32),
            jax.ShapeDtypeStruct((held, order, order), BF16),
            jax.ShapeDtypeStruct((grad_rows * blocks, order), BF16),
        ),
        in_specs=[vmem] * 3,
        out_specs=(any_space,) * 3,
        scratch_shapes=[
            pltpu.VMEM((grad_rows * blocks, order), BF16),
            pltpu.SemaphoreType.DMA((2 + CHUNKS,)),
        ],
        compiler_params=pltpu.CompilerParams(
            vmem_limit_bytes=grad_rows * blocks * order * 2 + (2 << 20)
        ),
    )(covariance, new_inverse, wide)
    return covariance, new_inverse, precond.reshape(grad_rows, blocks, order)


def solution(mesh):
    return jax.shard_map(
        local,
        mesh=mesh,
        in_specs=(
            P("rep", "mp", None),
            P(("mp", "rep")),
            P(("mp", "rep")),
            P(("mp", "rep"), None, None),
            P("rep", "mp", None),
        ),
        out_specs=(
            P(("mp", "rep"), None, None),
            P(("mp", "rep"), None, None),
            P("rep", "mp", None),
        ),
        check_vma=False,
    )
```

```python
import functools
import math

import jax
import jax.numpy as jnp
from jax import lax
from jax.experimental import pallas as pl
from jax.experimental.pallas import tpu as pltpu
from jax.sharding import PartitionSpec as P

ITERS = 5
CHUNKS = 2
LOADS = 2
MESH = pl.DeviceIdType.MESH
F32 = jnp.float32
BF16 = jnp.bfloat16


def split(x):
    high = x.astype(BF16)
    return high, (x - high.astype(F32)).astype(BF16)


def dot3(lhs, rhs):
    lh, ll = lhs
    rh, rl = rhs
    mm = functools.partial(jnp.dot, preferred_element_type=F32)
    return mm(lh, rh) + (mm(lh, rl) + mm(ll, rh))


def partner(me, step, n):
    if n & (n - 1):
        return lax.rem(me + step, n), lax.rem(me + n - step, n)
    other = me
    bit = 1
    while bit < n:
        if step & bit:
            other = other + bit * (1 - 2 * lax.rem(me // bit, 2))
        bit *= 2
    return other, other


def general_kernel(
    n,
    held,
    groups,
    tokens_all,
    acts_hbm,
    refresh_ref,
    damping_ref,
    old_hbm,
    grads_hbm,
    cov_ref,
    inv_ref,
    pre_f,
    acts_v,
    grads_v,
    old_v,
    acts_f,
    grads_f,
    own_f,
    out_buf,
    in_buf,
    gathered,
    load_sem,
    rs_send,
    rs_recv,
    ag_send,
    ag_recv,
):
    me = lax.axis_index("rep")
    blocks = n * held
    order = inv_ref.shape[-1]
    half = order // 2
    rows = acts_v.shape[0] // blocks

    barrier = pltpu.get_barrier_semaphore()
    for step in range(1, n):
        pl.semaphore_signal(
            barrier, inc=1, device_id={"rep": partner(me, step, n)[0]}, device_id_type=MESH
        )

    piece = acts_v.shape[0] // LOADS
    loads = [
        pltpu.make_async_copy(acts_hbm.at[pl.ds(c * piece, piece)], acts_v.at[pl.ds(c * piece, piece)], load_sem.at[3 + c])
        for c in range(LOADS)
    ] + [
        pltpu.make_async_copy(grads_hbm, grads_v, load_sem.at[1]),
        pltpu.make_async_copy(old_hbm, old_v, load_sem.at[2]),
    ]
    for load in loads:
        load.start()

    row_id = lax.broadcasted_iota(jnp.int32, (half, half), 0)
    col_id = lax.broadcasted_iota(jnp.int32, (half, half), 1)
    upper = col_id >= row_id
    on_diag = col_id == row_id

    def widen(source, target):
        for tile in range(order // 128):
            target[tile] = source[:, tile * 128 : (tile + 1) * 128].astype(F32)

    def take(source, block):
        return jnp.concatenate(
            [
                source[tile, pl.ds(block, rows, stride=blocks), :]
                for tile in range(order // 128)
            ],
            axis=1,
        ).astype(BF16)

    def gram(block):
        part = take(acts_f, block)
        full = lax.dot_general(
            part, part, (((0,), (0,)), ((), ())), preferred_element_type=F32
        )
        low = full[half:, half:]
        last = jnp.sum(jnp.where(on_diag, low, 0.0), axis=0, keepdims=True)
        return full[:half, half:], jnp.where(upper, full[:half, :half], low), last

    for c in range(LOADS):
        loads[c].wait()
        part = pl.ds(c * piece, piece)
        for tile in range(order // 128):
            acts_f[tile, part, :] = acts_v[part, tile * 128 : (tile + 1) * 128].astype(F32)

    rs = {}
    greeted = False
    steps = list(range(n - 1, 0, -1))
    for slot in range(held):
        for step in steps:
            target = partner(me, step, n)[0]
            cross, packed, last = gram(target * held + slot)
            place = out_buf.at[step - 1, slot]
            place[:half, :] = cross.astype(BF16)
            place[half : 2 * half, :] = packed.astype(BF16)
            place[2 * half :, :] = jnp.broadcast_to(last, (16, half)).astype(BF16)
            if not greeted:
                pl.semaphore_wait(barrier, n - 1)
                greeted = True
            copy = pltpu.make_async_remote_copy(
                src_ref=place,
                dst_ref=in_buf.at[step - 1, slot],
                send_sem=rs_send.at[step - 1, slot],
                recv_sem=rs_recv.at[step - 1, slot],
                device_id={"rep": target},
                device_id_type=MESH,
            )
            copy.start()
            rs[step, slot] = copy
        cross, packed, last = gram(me * held + slot)
        own_f[slot, :half, :] = cross
        own_f[slot, half : 2 * half, :] = packed
        own_f[slot, 2 * half :, :] = jnp.broadcast_to(last, (8, half))

    loads[LOADS].wait()
    widen(grads_v, grads_f)
    loads[LOADS + 1].wait()

    eye = jnp.where(
        lax.broadcasted_iota(jnp.int32, (order, order), 0)
        == lax.broadcasted_iota(jnp.int32, (order, order), 1),
        1.0,
        0.0,
    ).astype(F32)

    ag = {}

    def ship(key, source, target, step, sem):
        copy = pltpu.make_async_remote_copy(
            src_ref=source,
            dst_ref=target,
            send_sem=ag_send.at[sem],
            recv_sem=ag_recv.at[sem],
            device_id={"rep": partner(me, step, n)[0]},
            device_id_type=MESH,
        )
        copy.start()
        ag[key] = copy

    def refresh_block(slot):
        total = own_f[slot]
        total_cross, total_packed, total_last = (
            total[:half],
            total[half : 2 * half],
            total[2 * half : 2 * half + 1],
        )
        for step in steps:
            rs[step, slot].wait_recv()
            came = in_buf[step - 1, slot].astype(F32)
            total_cross = total_cross + came[:half]
            total_packed = total_packed + came[half : 2 * half]
            total_last = total_last + came[2 * half : 2 * half + 1]
        scale = 1.0 / tokens_all
        flipped = total_packed.T
        first = jnp.where(upper, total_packed, flipped)
        second = jnp.where(
            on_diag,
            jnp.broadcast_to(total_last, (half, half)),
            jnp.where(upper, flipped, total_packed),
        )
        covariance = (
            jnp.concatenate(
                [
                    jnp.concatenate([first, total_cross], axis=1),
                    jnp.concatenate([total_cross.T, second], axis=1),
                ],
                axis=0,
            )
            * scale
        )
        cov_ref[slot] = covariance
        matrix = covariance + damping_ref[slot] * eye
        bound = jnp.max(jnp.sum(jnp.abs(matrix), axis=0, keepdims=True), axis=1, keepdims=True)
        inverse_bound = 1.0 / bound
        residual = eye - matrix * inverse_bound
        series = eye + residual
        power = split(residual)
        power = split(dot3(power, power))
        for iteration in range(2, ITERS):
            left = split(series)
            square = dot3(power, power)
            series = series + dot3(left, power)
            power = split(square)
        series = series + dot3(split(series), power)
        approx = (series * inverse_bound).astype(BF16)
        due = jnp.full((order, order), refresh_ref[slot], jnp.int32) != groups
        chosen = jnp.where(due, approx, old_v[slot])
        inv_ref[slot] = chosen
        gathered[0, slot] = chosen
        for step in steps:
            ship(
                (slot, step),
                gathered.at[0, slot],
                gathered.at[step, slot],
                step,
                slot * n + step,
            )

    def apply(step, slot):
        block = partner(me, step, n)[1] * held + slot
        result = jnp.dot(
            take(grads_f, block), gathered[step, slot], preferred_element_type=F32
        )
        for tile in range(order // 128):
            pre_f[tile, pl.ds(block, rows, stride=blocks), :] = result[
                :, tile * 128 : (tile + 1) * 128
            ]

    for slot in range(held):
        refresh_block(slot)
    for slot in range(held):
        apply(0, slot)
    for slot in range(held):
        for step in steps:
            ag[slot, step].wait_recv()
            apply(step, slot)
    for copy in rs.values():
        copy.wait_send()
    for copy in ag.values():
        copy.wait_send()


def square_kernel(
    held,
    groups,
    tokens_all,
    acts_hbm,
    refresh_hbm,
    damping_hbm,
    old_hbm,
    grads_hbm,
    cov_ref,
    inv_ref,
    pre_f,
    refresh_s,
    damping_s,
    acts_v,
    grads_v,
    old_v,
    acts_f,
    grads_f,
    grads_b,
    own_f,
    mid_f,
    sum_out,
    sum_in,
    early_own,
    early_in,
    late_own,
    late_in,
    sent_bytes,
    load_sem,
    send_sem,
    recv_sem,
):
    n = 4
    me = lax.axis_index("rep")
    blocks = n * held
    order = inv_ref.shape[-1]
    half = order // 2
    rows = acts_v.shape[0] // blocks
    grad_rows = grads_v.shape[0] // blocks
    peer = [partner(me, step, n)[0] for step in range(n)]

    barrier = pltpu.get_barrier_semaphore()
    for step in (1, 2):
        pl.semaphore_signal(
            barrier, inc=1, device_id={"rep": peer[step]}, device_id_type=MESH
        )

    piece = acts_v.shape[0] // LOADS
    acts_loads = [
        pltpu.make_async_copy(
            acts_hbm.at[pl.ds(c * piece, piece)],
            acts_v.at[pl.ds(c * piece, piece)],
            load_sem.at[4 + c],
        )
        for c in range(LOADS)
    ]
    old_load = pltpu.make_async_copy(old_hbm, old_v, load_sem.at[0])
    grads_load = pltpu.make_async_copy(grads_hbm, grads_v, load_sem.at[1])
    refresh_load = pltpu.make_async_copy(refresh_hbm, refresh_s, load_sem.at[2])
    damping_load = pltpu.make_async_copy(damping_hbm, damping_s, load_sem.at[3])
    for load in acts_loads:
        load.start()

    landings = {}

    def copy_of(landing, source, target, step):
        return pltpu.make_async_remote_copy(
            src_ref=source,
            dst_ref=target,
            send_sem=send_sem.at[0],
            recv_sem=recv_sem.at[landings.setdefault(landing, len(landings))],
            device_id={"rep": peer[step]},
            device_id_type=MESH,
        )

    def send(landing, source, target, step):
        copy_of(landing, source, target, step).start()

    def arrived(landing, target):
        copy_of(landing, target, target, 1).wait_recv()

    row_id = lax.broadcasted_iota(jnp.int32, (half, half), 0)
    col_id = lax.broadcasted_iota(jnp.int32, (half, half), 1)
    upper = col_id >= row_id
    on_diag = col_id == row_id

    def widen(source, target, part):
        for tile in range(order // 128):
            target[tile, part, :] = source[part, tile * 128 : (tile + 1) * 128].astype(F32)

    def take(source, block, count):
        return jnp.concatenate(
            [
                source[tile, pl.ds(block, count, stride=blocks), :]
                for tile in range(order // 128)
            ],
            axis=1,
        ).astype(BF16)

    def diagonal(square):
        return jnp.sum(jnp.where(on_diag, square, 0.0), axis=0, keepdims=True)

    def gram(block):
        part = take(acts_f, block, rows)
        full = lax.dot_general(
            part, part, (((0,), (0,)), ((), ())), preferred_element_type=F32
        )
        low = full[half:, half:]
        return full[:half, half:], jnp.where(upper, full[:half, :half], low), diagonal(low)

    def keep(place, parts):
        cross, packed, last = parts
        place[:half, :] = cross.astype(place.dtype)
        place[half : 2 * half, :] = packed.astype(place.dtype)
        place[2 * half :, :] = jnp.broadcast_to(
            last, (place.shape[0] - 2 * half, half)
        ).astype(place.dtype)

    def parts_of(value):
        value = value.astype(F32)
        return value[:half], value[half : 2 * half], value[2 * half : 2 * half + 1]

    def add(*terms):
        return tuple(sum(entries[1:], entries[0]) for entries in zip(*terms))

    def axes(slot):
        return (1, 2) if slot % 2 == 0 else (2, 1)

    quarter = half // 2
    early_parts = {
        "d": (pl.ds(0, half), pl.ds(0, quarter), pl.ds(quarter, quarter)),
        "e": (pl.ds(half, half), pl.ds(half, quarter), pl.ds(half + quarter, quarter)),
    }

    def early_send():
        for kind in ("d", "e"):
            for step in (1, 2):
                source = old_hbm.at[:, pl.ds(half, half), pl.ds(0, half)] if kind == "d" else early_own
                send(("early", step), source, early_in.at[step - 1, :, early_parts[kind][0]], step)

    def early_relay():
        for step in (1, 2):
            arrived(("early", step), early_in.at[step - 1])
            for kind in ("d", "e"):
                part = early_parts[kind][step]
                send(
                    ("early", 3),
                    early_in.at[step - 1, :, part],
                    early_in.at[2, :, part],
                    3 - step,
                )

    for c in range(LOADS):
        acts_loads[c].wait()
        if c == LOADS - 1:
            for load in (old_load, refresh_load, damping_load, grads_load):
                load.start()
        widen(acts_v, acts_f, pl.ds(c * piece, piece))

    def pack_old():
        old_load.wait()
        for slot in range(held):
            old = old_v[slot].astype(F32)
            early_own[slot] = jnp.where(upper, old[half:, half:], old[:half, :half]).astype(BF16)

    for stage in (0, 1):
        for slot in range(held):
            near = axes(slot)[0]
            keep(sum_out.at[slot, stage], gram(peer[3 if stage == 0 else near] * held + slot))
            if stage == 0 and slot == 0:
                pl.semaphore_wait(barrier, 2)
            landing = ("pass", slot) if stage == 0 else "sums"
            send(landing, sum_out.at[slot, stage], sum_in.at[stage, slot], near)
    for slot in range(held):
        keep(mid_f.at[slot], gram(peer[axes(slot)[1]] * held + slot))
    for slot in range(held):
        keep(own_f.at[slot], gram(me * held + slot))
    old_load.wait()
    for slot in range(held):
        old = old_v[slot].astype(F32)
        early_own[slot] = jnp.where(upper, old[half:, half:], old[:half, :half]).astype(BF16)

    for slot in range(held):
        arrived(("pass", slot), sum_in.at[0, slot])
        keep(sum_out.at[slot, 2], add(parts_of(mid_f[slot]), parts_of(sum_in[0, slot])))
        send("sums", sum_out.at[slot, 2], sum_in.at[2, slot], axes(slot)[1])
    early_send()

    grads_load.wait()
    widen(grads_v, grads_f, pl.ds(0, grads_v.shape[0]))
    for step in range(n):
        for slot in range(held):
            grads_b[step * held + slot] = take(grads_f, peer[step] * held + slot, grad_rows)

    one = functools.partial(jnp.dot, preferred_element_type=F32)
    eye = jnp.where(
        lax.broadcasted_iota(jnp.int32, (order, order), 0)
        == lax.broadcasted_iota(jnp.int32, (order, order), 1),
        1.0,
        0.0,
    ).astype(F32)
    refresh_load.wait()
    damping_load.wait()

    cut = (order + 16) // 32 * 16
    top, bottom = pl.ds(0, cut), pl.ds(cut, order + 16 - cut)

    def summed(slot):
        return add(parts_of(own_f[slot]), parts_of(sum_in[1, slot]), parts_of(sum_in[2, slot]))

    def assemble(slot, parts):
        cross, packed, last = (part * (1.0 / tokens_all) for part in parts)
        flipped = packed.T
        first = jnp.where(upper, packed, flipped)
        second = jnp.where(
            on_diag,
            jnp.broadcast_to(last, (half, half)),
            jnp.where(upper, flipped, packed),
        )
        covariance = jnp.concatenate(
            [
                jnp.concatenate([first, cross], axis=1),
                jnp.concatenate([cross.T, second], axis=1),
            ],
            axis=0,
        )
        cov_ref[slot] = covariance
        matrix = covariance + damping_s[slot] * eye
        bound = jnp.max(jnp.sum(jnp.abs(matrix), axis=0, keepdims=True), axis=1, keepdims=True)
        inverse_bound = 1.0 / bound
        residual = eye - matrix * inverse_bound
        pair = split(matrix)
        square = dot3(pair, pair) * (inverse_bound * inverse_bound)
        return inverse_bound, residual, split(square + (residual - matrix * inverse_bound))

    def newton(slots):
        arrived("sums", sum_in.at[pl.ds(1, 2)])
        bounds, residuals, power = zip(*(assemble(slot, summed(slot)) for slot in slots))
        many = range(len(slots))
        series = [eye + residual for residual in residuals]
        for iteration in range(2, ITERS):
            last_one = iteration == ITERS - 1
            square = [one(item[0], item[0]) if last_one else dot3(item, item) for item in power]
            series = [series[i] + one(series[i].astype(BF16), power[i][0]) for i in many]
            power = [(item.astype(BF16),) if last_one else split(item) for item in square]
        for i in many:
            total = series[i] + one(series[i].astype(BF16), power[i][0])
            finish(slots[i], total * bounds[i])
            late_first(slots[i])

    def finish(slot, approx):
        due = jnp.full((order, order), refresh_s[slot], jnp.int32) != groups
        chosen = jnp.where(due, approx.astype(BF16), old_v[slot])
        inv_ref[slot] = chosen
        chosen = chosen.astype(F32)
        low = chosen[half:, half:]
        late_own[slot, :half, :] = chosen[:half, half:].astype(BF16)
        late_own[slot, half:order, :] = jnp.where(upper, chosen[:half, :half], low).astype(BF16)
        due_row = jnp.where(jnp.full((8, half), refresh_s[slot], jnp.int32) != groups, 1.0, 0.0)
        late_own[slot, order:, :] = jnp.concatenate(
            [jnp.broadcast_to(diagonal(low), (8, half)), due_row], axis=0
        ).astype(BF16)

    def late_send(landing, slot, step, part):
        send(landing, late_own.at[slot, part], late_in.at[step - 1, slot, part], step)

    def late_first(slot):
        late_send(("first", slot, 1), slot, 1, top)
        late_send(("first", slot, 2), slot, 2, bottom)

    def late_relay(slot):
        for step, part in ((1, top), (2, bottom)):
            arrived(("first", slot, step), late_in.at[step - 1, slot, part])
            send(
                ("relay", slot),
                late_in.at[step - 1, slot, part],
                late_in.at[2, slot, part],
                3 - step,
            )

    def multiply(step, slot, inverse):
        block = peer[step] * held + slot
        result = jnp.dot(grads_b[step * held + slot], inverse, preferred_element_type=F32)
        for tile in range(order // 128):
            pre_f[tile, pl.ds(block, grad_rows, stride=blocks), :] = result[
                :, tile * 128 : (tile + 1) * 128
            ]

    def apply(step, slot):
        late = late_in[step - 1, slot].astype(F32)
        early = early_in[step - 1, slot].astype(F32)
        cross, packed = late[:half], late[half:order]
        last, flag = late[order : order + 1], late[order + 8 : order + 9]
        due = jnp.broadcast_to(flag, (half, half)) > 0.5
        other = jnp.where(
            due,
            jnp.where(on_diag, jnp.broadcast_to(last, (half, half)), packed.T),
            early[half:],
        )
        inverse = jnp.concatenate(
            [
                jnp.concatenate([jnp.where(upper, packed, other), cross], axis=1),
                jnp.concatenate(
                    [jnp.where(due, cross.T, early[:half]), jnp.where(upper, other, packed)], axis=1
                ),
            ],
            axis=0,
        ).astype(BF16)
        multiply(step, slot, inverse)

    newton(list(range(held)))
    for step, part in ((1, bottom), (2, top)):
        send(("rest", step), late_own.at[:, part], late_in.at[step - 1, :, part], step)
    early_relay()
    for slot in range(held):
        multiply(0, slot, inv_ref[slot])
    for slot in range(held):
        late_relay(slot)
    arrived(("early", 3), early_in.at[2])
    for step, part in ((1, bottom), (2, top)):
        arrived(("rest", step), late_in.at[step - 1, :, part])
        for slot in range(held):
            apply(step, slot)
    for slot in range(held):
        arrived(("relay", slot), late_in.at[2, slot])
        apply(3, slot)
    pltpu.make_async_copy(sent_bytes, sent_bytes, send_sem.at[0]).wait()


def deliver(cov_v, inv_v, wide, cov_hbm, inv_hbm, pre_hbm, narrow, sem):
    copies = [
        pltpu.make_async_copy(cov_v, cov_hbm, sem.at[0]),
        pltpu.make_async_copy(inv_v, inv_hbm, sem.at[1]),
    ]
    for copy in copies:
        copy.start()
    size = narrow.shape[0] // CHUNKS
    for chunk in range(CHUNKS):
        part = pl.ds(chunk * size, size)
        for tile in range(wide.shape[0]):
            narrow[part, tile * 128 : (tile + 1) * 128] = wide[tile, part, :].astype(BF16)
        copy = pltpu.make_async_copy(narrow.at[part], pre_hbm.at[part], sem.at[2 + chunk])
        copy.start()
        copies.append(copy)
    for copy in copies:
        copy.wait()


def local(acts, refresh, damping, old_inverse, grads):
    n = lax.axis_size("rep")
    groups = lax.axis_size("mp")
    rows, blocks, order = acts.shape
    grad_rows = grads.shape[0]
    held = refresh.shape[0]
    half = order // 2
    tiles = order // 128
    any_space = pl.BlockSpec(memory_space=pltpu.HBM)
    smem = pl.BlockSpec(memory_space=pltpu.SMEM)
    vmem = pl.BlockSpec(memory_space=pltpu.VMEM)
    wide_scratch = [
        pltpu.VMEM((rows * blocks, order), BF16),
        pltpu.VMEM((grad_rows * blocks, order), BF16),
        pltpu.VMEM((held, order, order), BF16),
        pltpu.VMEM((tiles, rows * blocks, 128), F32),
        pltpu.VMEM((tiles, grad_rows * blocks, 128), F32),
    ]
    if n == 4:
        body = functools.partial(square_kernel, held, groups, rows * n)
        scratch = (
            [pltpu.SMEM((held,), jnp.int32), pltpu.SMEM((held,), F32)]
            + wide_scratch
            + [
                pltpu.VMEM((blocks, grad_rows, order), BF16),
                pltpu.VMEM((held, order + 8, half), F32),
                pltpu.VMEM((held, order + 8, half), F32),
                pltpu.VMEM((held, 3, order + 16, half), BF16),
                pltpu.VMEM((3, held, order + 16, half), BF16),
                pltpu.VMEM((held, half, half), BF16),
                pltpu.VMEM((3, held, order, half), BF16),
                pltpu.VMEM((held, order + 16, half), BF16),
                pltpu.VMEM((3, held, order + 16, half), BF16),
                pltpu.VMEM((held * (6 * (order + 16) + 3 * order), half), BF16),
                pltpu.SemaphoreType.DMA((4 + LOADS,)),
                pltpu.SemaphoreType.DMA((1,)),
                pltpu.SemaphoreType.DMA((6 + 4 * held,)),
            ]
        )
        small = any_space
    else:
        body = functools.partial(general_kernel, n, held, groups, rows * n)
        scratch = wide_scratch + [
            pltpu.VMEM((held, order + 8, half), F32),
            pltpu.VMEM((n - 1, held, order + 16, half), BF16),
            pltpu.VMEM((n - 1, held, order + 16, half), BF16),
            pltpu.VMEM((n, held, order, order), BF16),
            pltpu.SemaphoreType.DMA((3 + LOADS,)),
            pltpu.SemaphoreType.DMA((n - 1, held)),
            pltpu.SemaphoreType.DMA((n - 1, held)),
            pltpu.SemaphoreType.DMA((held * n,)),
            pltpu.SemaphoreType.DMA((held * n,)),
        ]
        small = smem
    need = sum(
        math.prod(item.shape) * jnp.dtype(item.dtype).itemsize
        for item in scratch
        if item.memory_space == pltpu.VMEM
    )
    covariance, new_inverse, wide = pl.pallas_call(
        body,
        out_shape=(
            pltpu.VMEM((held, order, order), F32),
            pltpu.VMEM((held, order, order), BF16),
            pltpu.VMEM((tiles, grad_rows * blocks, 128), F32),
        ),
        in_specs=[any_space, small, small, any_space, any_space],
        out_specs=(vmem, vmem, vmem),
        scratch_shapes=scratch,
        compiler_params=pltpu.CompilerParams(
            collective_id=0, has_side_effects=True, vmem_limit_bytes=need + (8 << 20)
        ),
    )(
        pltpu.with_memory_space_constraint(acts.reshape(rows * blocks, order), pltpu.HBM),
        pltpu.with_memory_space_constraint(refresh, pltpu.HBM),
        pltpu.with_memory_space_constraint(damping, pltpu.HBM),
        pltpu.with_memory_space_constraint(old_inverse, pltpu.HBM),
        pltpu.with_memory_space_constraint(grads.reshape(grad_rows * blocks, order), pltpu.HBM),
    )
    covariance, new_inverse, precond = pl.pallas_call(
        deliver,
        out_shape=(
            jax.ShapeDtypeStruct((held, order, order), F32),
            jax.ShapeDtypeStruct((held, order, order), BF16),
            jax.ShapeDtypeStruct((grad_rows * blocks, order), BF16),
        ),
        in_specs=[vmem] * 3,
        out_specs=(any_space,) * 3,
        scratch_shapes=[
            pltpu.VMEM((grad_rows * blocks, order), BF16),
            pltpu.SemaphoreType.DMA((2 + CHUNKS,)),
        ],
        compiler_params=pltpu.CompilerParams(
            vmem_limit_bytes=grad_rows * blocks * order * 2 + (2 << 20)
        ),
    )(covariance, new_inverse, wide)
    return covariance, new_inverse, precond.reshape(grad_rows, blocks, order)


def solution(mesh):
    return jax.shard_map(
        local,
        mesh=mesh,
        in_specs=(
            P("rep", "mp", None),
            P(("mp", "rep")),
            P(("mp", "rep")),
            P(("mp", "rep"), None, None),
            P("rep", "mp", None),
        ),
        out_specs=(
            P(("mp", "rep"), None, None),
            P(("mp", "rep"), None, None),
            P("rep", "mp", None),
        ),
        check_vma=False,
    )
```
